256 devices in a mesh: gx: 32 (over y, x, core), gy: 8 (over z).
Axes of the slice: x: 4, y: 4, z: 8, core: 2. Of those that a mesh axis runs over, the one named last changes fastest.
Arguments:
- value_field: float32 [128, 64, 8, 1024], P('gx', 'gy'), may hold values from -6 to 6
- obstacle: float32 [128, 64, 8, 1024], P('gx', 'gy'), may hold values from -4 to 4
- drift_field: float32 [128, 64, 2], P('gx', 'gy'), may hold values from -9 to 9
Outputs:
- value_next: float32 [128, 64, 8, 1024], P('gx', 'gy')
- steps_taken: float32 [4], replicated
The draws below stay inside these ranges and needn't reach their ends.
All inputs are finite; a program needn't handle non-finite values.
Results may differ from the reference program's by a relative error of at most 0.00002.
Values sent between devices are 32-bit elements; how exact they have to be, the bound alone decides.
A program may use at most 128 MiB of HBM per device.

```python
import math
import jax
import jax.numpy as jnp
from jax import lax

NTH = 8
NV = 16
NW = 64
ITERS = 4
NX = 128
NY = 64


def draw_value_field(key, part):
    extent = (NX, NY, NTH, NV * NW)
    first_pos = jnp.arange(NX).astype(jnp.float32) / max(NX - 1, 1)
    noise_field = jnp.clip(jax.random.normal(key, extent, jnp.float32), -4.0, 4.0)
    amplitude = 0.5 * 3.0 ** first_pos
    return amplitude[:, None, None, None] * noise_field


def draw_drift_field(key, part):
    extent = (NX, NY, 2)
    second_pos = jnp.arange(NY).astype(jnp.float32) / max(NY - 1, 1)
    noise_field = jnp.clip(jax.random.normal(key, extent, jnp.float32), -3.0, 3.0)
    amplitude = 0.3 * 10.0 ** second_pos
    return amplitude[None, :, None] * noise_field


def block_levels(rng, shape, cuts, least, high):
    level, own = 1.0, jax.random.fold_in(rng, 6)
    for position, shards_of in cuts:
        heights = jnp.exp(jax.random.uniform(jax.random.fold_in(own, position), (shards_of,), jnp.float32, least / len(cuts), high / len(cuts)))
        level = level * jnp.repeat(heights, shape[position] // shards_of).reshape([-1 if axis == position else 1 for axis in range(len(shape))])
    return level


def bell_draw(rng, shape, scale, bound, pieces=(), kind=jnp.bfloat16):
    result = scale * jax.random.normal(rng, shape, jnp.float32)
    if pieces:
        result = result * block_levels(rng, shape, pieces, -0.22, 0.18)
    return jnp.clip(result, -bound, bound).astype(kind)


def setup_inputs(seed: int = 0) -> dict:
    splits = jax.random.split(jax.random.key(seed), 4)
    return {
        "value_field": draw_value_field(jax.random.fold_in(splits[3], 71), 0),
        "obstacle": bell_draw(splits[1], (NX, NY, NTH, NV * NW), 1.0, 4.0, ((0, 32), (1, 8)), jnp.float32),
        "drift_field": draw_drift_field(jax.random.fold_in(splits[3], 71), 0),
    }


SPACE_STEP = 0.5
SPEED_BASE = 1.0
SPEED_STEP = 0.2
TURN_LIMIT = 0.25
EFFORT_COST = 10.0
COURANT = 0.9


def grid_lanes():
    heading = jnp.arange(NTH, dtype=jnp.int32).astype(jnp.float32) * (2.0 * math.pi / NTH)
    lane_index = jnp.arange(NV * NW, dtype=jnp.int32)
    speed_row = SPEED_BASE + (lane_index // NW).astype(jnp.float32) * SPEED_STEP
    turning = -1.0 + ((lane_index % NW).astype(jnp.float32) + 0.5) * (2.0 / NW)
    cosine_speed = jnp.cos(heading)[:, None] * speed_row[None, :]
    sine_speed = jnp.sin(heading)[:, None] * speed_row[None, :]
    return cosine_speed, sine_speed, turning


def rate_field(drift_part):
    cosine_speed, sine_speed, turning = grid_lanes()
    east_rate = cosine_speed + drift_part[:, :, 0][:, :, None, None]
    north_rate = sine_speed + drift_part[:, :, 1][:, :, None, None]
    head_step = 2.0 * math.pi / NTH
    turn_step = 2.0 / NW
    return jnp.abs(east_rate) / SPACE_STEP + jnp.abs(north_rate) / SPACE_STEP + jnp.abs(turning) / head_step + TURN_LIMIT / turn_step


def advance(extended, drift_part, barrier, time_step, slope_rate):
    center = extended[1:-1, 1:-1]
    east_plus = (extended[2:, 1:-1] - center) / SPACE_STEP
    east_minus = (center - extended[:-2, 1:-1]) / SPACE_STEP
    north_plus = (extended[1:-1, 2:] - center) / SPACE_STEP
    north_minus = (center - extended[1:-1, :-2]) / SPACE_STEP
    head_step = 2.0 * math.pi / NTH
    turn_step = 2.0 / NW
    head_plus = (jnp.roll(center, -1, axis=2) - center) / head_step
    head_minus = (center - jnp.roll(center, 1, axis=2)) / head_step
    speed_diff = (center[..., NW:] - center[..., :-NW]) / SPEED_STEP
    speed_plus = jnp.concatenate([speed_diff, speed_diff[..., -NW:]], axis=3)
    speed_minus = jnp.concatenate([speed_diff[..., :NW], speed_diff], axis=3)
    turn_diff = (center[..., 1:] - center[..., :-1]) / turn_step
    padding = jnp.zeros_like(turn_diff[..., :1])
    forward = jnp.concatenate([turn_diff, padding], axis=3)
    backward = jnp.concatenate([padding, turn_diff], axis=3)
    lane_pos = jnp.arange(center.shape[3], dtype=jnp.int32) % NW
    turn_plus = jnp.where(lane_pos == NW - 1, backward, forward)
    turn_minus = jnp.where(lane_pos == 0, forward, backward)
    cosine_speed, sine_speed, turning = grid_lanes()
    east_rate = cosine_speed + drift_part[:, :, 0][:, :, None, None]
    north_rate = sine_speed + drift_part[:, :, 1][:, :, None, None]
    speed_mean = 0.5 * (speed_plus + speed_minus)
    hamiltonian = (east_rate * (0.5 * (east_plus + east_minus))
                   + north_rate * (0.5 * (north_plus + north_minus))
                   + turning * (0.5 * (head_plus + head_minus))
                   + speed_mean * speed_mean / (2.0 * EFFORT_COST)
                   + TURN_LIMIT * jnp.abs(0.5 * (turn_plus + turn_minus)))
    damping = (jnp.abs(east_rate) * (0.5 * (east_plus - east_minus))
               + jnp.abs(north_rate) * (0.5 * (north_plus - north_minus))
               + jnp.abs(turning) * (0.5 * (head_plus - head_minus))
               + slope_rate * (0.5 * (speed_plus - speed_minus))
               + TURN_LIMIT * (0.5 * (turn_plus - turn_minus)))
    return jnp.minimum(center + time_step * (hamiltonian + damping), barrier)


def extend_edges(source, axis):
    extent = source.shape[axis]
    low_edge = 2.0 * lax.slice_in_dim(source, 0, 1, axis=axis) - lax.slice_in_dim(source, 1, 2, axis=axis)
    high_edge = 2.0 * lax.slice_in_dim(source, extent - 1, extent, axis=axis) - lax.slice_in_dim(source, extent - 2, extent - 1, axis=axis)
    return jnp.concatenate([low_edge, source, high_edge], axis=axis)


def reference(value_field, obstacle, drift_field):
    row_numbers = jnp.arange(NX, dtype=jnp.int32)

    def row_rate(row_at):
        drift_part = lax.dynamic_slice_in_dim(drift_field, row_at, 1, 0)
        return jnp.max(rate_field(drift_part))

    rate_top = jnp.max(lax.map(row_rate, row_numbers))
    step_list = []
    current_value = value_field
    for step_index in range(ITERS):
        def row_slope(row_at):
            row_data = lax.dynamic_slice_in_dim(current_value, row_at, 1, 0)
            return jnp.max(jnp.abs(row_data[..., NW:] - row_data[..., :-NW]))

        top_slope = jnp.max(lax.map(row_slope, row_numbers)) / SPEED_STEP
        rate_bound = rate_top + top_slope / (EFFORT_COST * SPEED_STEP)
        time_step = COURANT / rate_bound
        padded = extend_edges(current_value, 0)

        def row_update(row_at):
            window = extend_edges(lax.dynamic_slice_in_dim(padded, row_at, 3, 0), 1)
            drift_part = lax.dynamic_slice_in_dim(drift_field, row_at, 1, 0)
            barrier = lax.dynamic_slice_in_dim(obstacle, row_at, 1, 0)
            return advance(window, drift_part, barrier, time_step, top_slope / EFFORT_COST)[0]

        current_value = lax.map(row_update, row_numbers)
        step_list.append(time_step)
    return current_value, jnp.stack(step_list)
```

```python
import functools
import math

import jax
import jax.numpy as jnp
import numpy as np
from jax import lax
from jax.experimental import pallas as pl
from jax.experimental.pallas import tpu as pltpu
from jax.sharding import PartitionSpec as P

NTH = 8
NV = 16
NW = 64
ITERS = 4
SPACE_STEP = 0.5
SPEED_BASE = 1.0
SPEED_STEP = 0.2
TURN_LIMIT = 0.25
EFFORT_COST = 10.0
COURANT = 0.9

LANES = 128
GROUPS = NV * NW // LANES
CHIP_X = 4
CHIP_Y = 4
CORES = 2
MESH = pl.DeviceIdType.MESH

HEAD_STEP = 2.0 * math.pi / NTH
TURN_STEP = 2.0 / NW
SCALE = TURN_LIMIT / TURN_STEP


def tables():
    heading = (np.arange(NTH, dtype=np.float32) * np.float32(2.0 * math.pi / NTH)).astype(np.float32)
    lane = np.arange(NV * NW)
    speed = (np.float32(SPEED_BASE) + (lane // NW).astype(np.float32) * np.float32(SPEED_STEP)).astype(np.float32)
    turning = (np.float32(-1.0) + ((lane % NW).astype(np.float32) + np.float32(0.5)) * np.float32(2.0 / NW)).astype(np.float32)
    cosine = np.cos(heading.astype(np.float64)).astype(np.float32)
    sine = np.sin(heading.astype(np.float64)).astype(np.float32)
    factor = np.float32(1.0 / (SPACE_STEP * SCALE))
    east = cosine[:, None] * speed[None, :] * factor
    north = sine[:, None] * speed[None, :] * factor
    turn = np.abs(turning[:LANES]) / np.float32(HEAD_STEP * SCALE)
    turn = np.broadcast_to(turn, (NTH, LANES))
    turn_top = float(np.max(np.abs(turning) / np.float32(HEAD_STEP)))
    return np.stack([east, north]).astype(np.float32), turn.astype(np.float32), turn_top


def kernel(nx, ny, bx, by, turn_top,
           drift, table, turn_table, value_hbm, barrier_hbm, out_hbm, steps_out,
           vb, ob, part_a, part_b, new, sent, got,
           in_sem, ob_sem, out_sem, halo_send, halo_recv, max_send, max_recv):
    me_x = lax.axis_index("gx")
    me_y = lax.axis_index("gy")
    chip = me_x // CORES
    core = me_x % CORES
    chip_y = chip // CHIP_X
    chip_x = chip % CHIP_X
    low_x, high_x = me_x > 0, me_x < nx - 1
    low_y, high_y = me_y > 0, me_y < ny - 1

    column = []
    for k in range(1, CORES * ny):
        other_core = lax.rem(core + k % CORES, CORES)
        other_y = lax.rem(me_y + k // CORES, ny)
        column.append((chip * CORES + other_core, other_y))
    plane = []
    for k in range(1, CHIP_Y * CHIP_X):
        other_cy = lax.rem(chip_y + k // CHIP_X, CHIP_Y)
        other_cx = lax.rem(chip_x + k % CHIP_X, CHIP_X)
        plane.append(((other_cy * CHIP_X + other_cx) * CORES + core, me_y))
    groups = (column, plane)
    sides = ((low_x, (me_x - 1, me_y)), (high_x, (me_x + 1, me_y)),
             (low_y, (me_x, me_y - 1)), (high_y, (me_x, me_y + 1)))

    loads = []
    for i in range(bx):
        copy = pltpu.make_async_copy(value_hbm.at[i], vb.at[0, i + 1, pl.ds(1, by)], in_sem.at[i])
        copy.start()
        loads.append(copy)
    ob_copy = pltpu.make_async_copy(barrier_hbm, ob, ob_sem)
    ob_copy.start()

    ready = pltpu.get_barrier_semaphore()
    for peer in plane + column:
        pl.semaphore_signal(ready, inc=1, device_id=peer, device_id_type=MESH)
    for exists, peer in sides:
        @pl.when(exists)
        def _(peer=peer):
            pl.semaphore_signal(ready, inc=1, device_id=peer, device_id_type=MESH)

    lane = lax.broadcasted_iota(jnp.int32, (NTH, LANES), 1)
    low_half = lane < NW
    in_row = lax.rem(lane, NW)
    first_turn = in_row == 0
    last_turn = in_row == NW - 1
    turn_up = in_row >= NW // 2
    turn_w = turn_table[...]

    def lanes_of(g):
        return slice(g * LANES, (g + 1) * LANES)

    def row_slope(vals, top):
        swapped = [pltpu.roll(v, NW, 1) for v in vals]
        for g in range(GROUPS):
            after = swapped[g + 1] if g + 1 < GROUPS else vals[g]
            ahead = jnp.where(low_half, swapped[g], after)
            top = jnp.maximum(top, jnp.abs(ahead - vals[g]))
        return top

    def one_row(top):
        return jnp.max(top, axis=0, keepdims=True)

    def rate_row(r, top):
        i, j = r // by, lax.rem(r, by)
        dx = drift[i, j * 2] * (1.0 / (SPACE_STEP * SCALE))
        dy = drift[i, j * 2 + 1] * (1.0 / (SPACE_STEP * SCALE))
        for g in range(GROUPS):
            east = table[0, :, lanes_of(g)] + dx
            north = table[1, :, lanes_of(g)] + dy
            top = jnp.maximum(top, jnp.abs(east) + jnp.abs(north))
        return top

    zero = jnp.zeros((NTH, LANES), jnp.float32)
    rate = lax.fori_loop(0, bx * by, rate_row, zero)

    top = zero
    for i in range(bx):
        loads[i].wait()

        def first_slope(j, top, i=i):
            return row_slope([vb[0, i + 1, j + 1, :, lanes_of(g)] for g in range(GROUPS)], top)

        top = lax.fori_loop(0, by, first_slope, top)

    expected = 2 * (len(plane))
    expected = expected + sum(jnp.where(exists, 1, 0) for exists, _ in sides)
    pl.semaphore_wait(ready, expected)

    def spread(step, stage):
        for k, peer in enumerate(groups[stage]):
            pltpu.make_async_remote_copy(
                src_ref=sent.at[step, stage], dst_ref=got.at[step, stage, k],
                send_sem=max_send.at[step, stage], recv_sem=max_recv.at[step, stage],
                device_id=peer, device_id_type=MESH).start()

    def collect(step, stage):
        pltpu.make_async_copy(got.at[step, stage], got.at[step, stage], max_recv.at[step, stage]).wait()
        best = sent[step, stage]
        for k in range(len(groups[stage])):
            best = jnp.maximum(best, got[step, stage, k])
        return best

    def halo_copy(step, side):
        inner = {0: (1, pl.ds(1, by)), 1: (bx, pl.ds(1, by)), 2: (pl.ds(1, bx), 1), 3: (pl.ds(1, bx), by)}[side]
        outer = {0: (bx + 1, pl.ds(1, by)), 1: (0, pl.ds(1, by)), 2: (pl.ds(1, bx), by + 1), 3: (pl.ds(1, bx), 0)}[side]
        return pltpu.make_async_remote_copy(
            src_ref=vb.at[(step,) + inner], dst_ref=vb.at[(step,) + outer],
            send_sem=halo_send.at[step, side], recv_sem=halo_recv.at[step, side],
            device_id=sides[side][1], device_id_type=MESH)

    opposite = (1, 0, 3, 2)

    def ghost(step, side):
        if side < 2:
            to, near, far = ((0, 1, 2), (bx + 1, bx, bx - 1))[side]

            def fill(j, carry):
                vb[step, to, j] = 2.0 * vb[step, near, j] - vb[step, far, j]
                return carry

            lax.fori_loop(1, by + 1, fill, 0)
        else:
            to, near, far = ((0, 1, 2), (by + 1, by, by - 1))[side - 2]

            def fill(i, carry):
                vb[step, i, to] = 2.0 * vb[step, i, near] - vb[step, i, far]
                return carry

            lax.fori_loop(1, bx + 1, fill, 0)

    rate_top = None
    for step in range(ITERS):
        row = one_row(top)
        if step == 0:
            rates = one_row(rate)
            row = jnp.maximum(row, pltpu.roll(row, NW, 1))
            rates = jnp.maximum(rates, pltpu.roll(rates, NW, 1))
            row = jnp.where(low_half[:1], row, rates)
        sent[step, 0] = row
        spread(step, 0)
        for side in range(4):
            @pl.when(sides[side][0])
            def _(side=side):
                halo_copy(step, side).start()

        def inner_terms(r, carry):
            i, j = r // by + 1, lax.rem(r, by) + 1
            vals = [vb[step, i, j, :, lanes_of(g)] for g in range(GROUPS)]
            swapped = [pltpu.roll(v, NW, 1) for v in vals]
            for g in range(GROUPS):
                v = vals[g]
                ahead = jnp.where(low_half, swapped[g], swapped[min(g + 1, GROUPS - 1)]) - v
                behind = jnp.where(low_half, swapped[max(g - 1, 0)], swapped[g]) - v
                if g == 0:
                    behind = jnp.where(low_half, -ahead, behind)
                if g == GROUPS - 1:
                    ahead = jnp.where(low_half, ahead, -behind)
                span = ahead - behind
                part_b[i - 1, j - 1, :, lanes_of(g)] = ahead + behind
                acc = span * span * (1.0 / (4.0 * SPEED_STEP * SPEED_STEP * 2.0 * EFFORT_COST * SCALE))
                right = pltpu.roll(v, LANES - 1, 1) - v
                left = pltpu.roll(v, 1, 1) - v
                acc += jnp.maximum(jnp.where(last_turn, -left, right), jnp.where(first_turn, -right, left))
                around = jnp.where(turn_up, pltpu.roll(v, NTH - 1, 0), pltpu.roll(v, 1, 0))
                acc += turn_w * (around - v)
                part_a[i - 1, j - 1, :, lanes_of(g)] = acc
            return carry

        lax.fori_loop(0, bx * by, inner_terms, 0)

        for side in range(4):
            @pl.when(jnp.logical_not(sides[side][0]))
            def _(side=side):
                ghost(step, side)

        sent[step, 1] = collect(step, 0)
        spread(step, 1)

        for side in range(4):
            @pl.when(sides[side][0])
            def _(side=side):
                rim = vb.at[(step,) + {0: (0, pl.ds(1, by)), 1: (bx + 1, pl.ds(1, by)),
                                       2: (pl.ds(1, bx), 0), 3: (pl.ds(1, bx), by + 1)}[side]]
                pltpu.make_async_copy(rim, rim, halo_recv.at[step, opposite[side]]).wait()

        def position_terms(r, carry):
            i, j = r // by + 1, lax.rem(r, by) + 1
            dx = drift[i - 1, (j - 1) * 2] * (1.0 / (SPACE_STEP * SCALE))
            dy = drift[i - 1, (j - 1) * 2 + 1] * (1.0 / (SPACE_STEP * SCALE))
            for g in range(GROUPS):
                s = lanes_of(g)
                v = vb[step, i, j, :, s]
                east = table[0, :, s] + dx
                north = table[1, :, s] + dy
                from_x = jnp.where(east > 0.0, vb[step, i + 1, j, :, s], vb[step, i - 1, j, :, s])
                from_y = jnp.where(north > 0.0, vb[step, i, j + 1, :, s], vb[step, i, j - 1, :, s])
                part_a[i - 1, j - 1, :, s] += jnp.abs(east) * (from_x - v) + jnp.abs(north) * (from_y - v)
            return carry

        lax.fori_loop(0, bx * by, position_terms, 0)

        best = collect(step, 1)
        if step == 0:
            ob_copy.wait()
            rate_top = jnp.max(jnp.where(low_half[:1], 0.0, best), axis=1, keepdims=True) * SCALE + turn_top + SCALE
            best = jnp.where(low_half[:1], best, 0.0)
        top_slope = jnp.max(best, axis=1, keepdims=True) / SPEED_STEP
        dt = COURANT / (rate_top + top_slope / (EFFORT_COST * SPEED_STEP))
        steps_out[step] = jnp.max(dt)
        weight_a = jnp.broadcast_to(SCALE * dt, (NTH, LANES))
        weight_b = jnp.broadcast_to(dt * (top_slope / EFFORT_COST) * (0.5 / SPEED_STEP), (NTH, LANES))

        def update(r, top):
            i, j = r // by, lax.rem(r, by)
            vals = []
            for g in range(GROUPS):
                s = lanes_of(g)
                moved = (vb[step, i + 1, j + 1, :, s] + weight_a * part_a[i, j, :, s]) + weight_b * part_b[i, j, :, s]
                moved = jnp.minimum(moved, ob[i, j, :, s])
                if step < ITERS - 1:
                    vb[step + 1, i + 1, j + 1, :, s] = moved
                else:
                    new[i, j, :, s] = moved
                vals.append(moved)
            return row_slope(vals, top) if step < ITERS - 1 else top

        if step < ITERS - 1:
            top = lax.fori_loop(0, bx * by, update, zero)
        else:
            stores = []
            for i in range(bx):
                lax.fori_loop(i * by, (i + 1) * by, update, zero)
                copy = pltpu.make_async_copy(new.at[i], out_hbm.at[i], out_sem.at[i])
                copy.start()
                stores.append(copy)

    for step in range(ITERS):
        for stage in range(2):
            pltpu.make_async_copy(got.at[step, stage], got.at[step, stage], max_send.at[step, stage]).wait()
        for side in range(4):
            @pl.when(sides[side][0])
            def _(side=side, step=step):
                halo_copy(step, side).wait_send()
    for copy in stores:
        copy.wait()


def per_device(nx, ny, value_field, obstacle, drift_field):
    bx, by = value_field.shape[:2]
    table, turn_table, turn_top = tables()
    shape = value_field.shape
    peers = CHIP_X * CHIP_Y - 1
    vmem = pl.BlockSpec(memory_space=pltpu.VMEM)
    smem = pl.BlockSpec(memory_space=pltpu.SMEM)
    hbm = pl.BlockSpec(memory_space=pl.ANY)
    dma = pltpu.SemaphoreType.DMA
    return pl.pallas_call(
        functools.partial(kernel, nx, ny, bx, by, turn_top),
        out_shape=(jax.ShapeDtypeStruct(shape, jnp.float32), jax.ShapeDtypeStruct((ITERS,), jnp.float32)),
        in_specs=[smem, vmem, vmem, hbm, hbm],
        out_specs=(hbm, smem),
        scratch_shapes=[
            pltpu.VMEM((ITERS, bx + 2, by + 2) + shape[2:], jnp.float32),
            pltpu.VMEM(shape, jnp.float32),
            pltpu.VMEM(shape, jnp.float32),
            pltpu.VMEM(shape, jnp.float32),
            pltpu.VMEM(shape, jnp.float32),
            pltpu.VMEM((ITERS, 2, 1, LANES), jnp.float32),
            pltpu.VMEM((ITERS, 2, peers, 1, LANES), jnp.float32),
            dma((bx,)), dma, dma((bx,)),
            dma((ITERS, 4)), dma((ITERS, 4)), dma((ITERS, 2)), dma((ITERS, 2)),
        ],
        compiler_params=pltpu.CompilerParams(
            collective_id=0, has_side_effects=True, vmem_limit_bytes=32 * 1024 * 1024),
        name="safe_set_steps",
    )(drift_field.reshape(bx, by * 2), table, turn_table, value_field, obstacle)


def solution(mesh):
    nx, ny = mesh.shape["gx"], mesh.shape["gy"]
    placed = (P("gx", "gy", None, None), P("gx", "gy", None, None), P("gx", "gy", None))
    return jax.shard_map(
        functools.partial(per_device, nx, ny),
        mesh=mesh,
        in_specs=placed,
        out_specs=(P("gx", "gy", None, None), P()),
        check_vma=False,
    )
```

```python
import functools
import math

import jax
import jax.numpy as jnp
import numpy as np
from jax import lax
from jax.experimental import pallas as pl
from jax.experimental.pallas import tpu as pltpu
from jax.sharding import PartitionSpec as P

NTH = 8
NV = 16
NW = 64
ITERS = 4
SPACE_STEP = 0.5
SPEED_BASE = 1.0
SPEED_STEP = 0.2
TURN_LIMIT = 0.25
EFFORT_COST = 10.0
COURANT = 0.9

LANES = 128
GROUPS = NV * NW // LANES
CHIP_X = 4
CHIP_Y = 4
CORES = 2
MESH = pl.DeviceIdType.MESH

HEAD_STEP = 2.0 * math.pi / NTH
TURN_STEP = 2.0 / NW
SCALE = TURN_LIMIT / TURN_STEP
POS = 1.0 / (SPACE_STEP * SCALE)

F32 = np.float32
HEADINGS = (np.arange(NTH, dtype=F32) * F32(HEAD_STEP)).astype(np.float64)
COSINES = [float(F32(c)) for c in np.cos(HEADINGS)]
SINES = [float(F32(s)) for s in np.sin(HEADINGS)]
TURN_TOP = float(F32((1.0 - 1.0 / NW)) / F32(HEAD_STEP))

PLANE = sorted(((a, b) for a in range(CHIP_Y) for b in range(CHIP_X) if (a, b) != (0, 0)),
               key=lambda t: -(min(t[0], CHIP_Y - t[0]) + min(t[1], CHIP_X - t[1])))


def lanes_of(g):
    return slice(g * LANES, (g + 1) * LANES)


def kernel(nx, ny, bx, by,
           drift_hbm, value_hbm, barrier_hbm, out_hbm, steps_out,
           vb, nat_v, nat_o, ob, part_a, part_b, table, drift, sent, got, rates, times,
           in_sem, ob_sem, drift_sem, out_sem, halo_send, halo_recv, max_send, max_recv):
    me_x = lax.axis_index("gx")
    me_y = lax.axis_index("gy")
    chip = me_x // CORES
    core = lax.rem(me_x, CORES)
    chip_y = chip // CHIP_X
    chip_x = lax.rem(chip, CHIP_X)
    plane = [((lax.rem(chip_y + a, CHIP_Y) * CHIP_X + lax.rem(chip_x + b, CHIP_X)) * CORES + core, me_y)
             for a, b in PLANE]
    column = []
    for k in [ny // 2] + [d for h in range(ny // 2 - 1, 0, -1) for d in (h, ny - h)] + [0]:
        for c in range(CORES - 1, -1, -1):
            if (k, c) != (0, 0):
                column.append((chip * CORES + lax.rem(core + c, CORES), lax.rem(me_y + k, ny)))
    groups = (plane, column)
    low_x, high_x = me_x > 0, me_x < nx - 1
    low_y, high_y = me_y > 0, me_y < ny - 1
    sides = ((low_x, (me_x - 1, me_y)), (high_x, (me_x + 1, me_y)),
             (low_y, (me_x, me_y - 1)), (high_y, (me_x, me_y + 1)))
    opposite = (1, 0, 3, 2)
    loads = []
    for i in range(bx):
        copy = pltpu.make_async_copy(value_hbm.at[i], nat_v.at[i], in_sem.at[i])
        copy.start()
        loads.append(copy)
    drift_copy = pltpu.make_async_copy(drift_hbm, drift, drift_sem)
    drift_copy.start()
    ob_copy = pltpu.make_async_copy(barrier_hbm, nat_o, ob_sem)
    ob_copy.start()

    ready = pltpu.get_barrier_semaphore()

    for peer in column + plane:
        pl.semaphore_signal(ready, inc=1, device_id=peer, device_id_type=MESH)
    beside_exists = jnp.where(core == 0, me_x - 1 >= 0, me_x + 1 < nx)
    beside = me_x - 1 + 2 * core

    @pl.when(beside_exists)
    def _():
        pl.semaphore_signal(ready, inc=1, device_id=(beside, me_y), device_id_type=MESH)

    lane = lax.broadcasted_iota(jnp.int32, (NTH, LANES), 1)
    low_half = lane < NW
    in_row = lax.rem(lane, NW)
    first_turn = in_row == 0
    last_turn = in_row == NW - 1
    turn_up = in_row >= NW // 2
    turning = -1.0 + (in_row.astype(jnp.float32) + 0.5) * (2.0 / NW)
    turn_w = jnp.abs(turning) * (1.0 / (HEAD_STEP * SCALE))
    zero = jnp.zeros((NTH, LANES), jnp.float32)

    heading = lax.broadcasted_iota(jnp.int32, (NTH, LANES), 0)
    cosine = jnp.full((NTH, LANES), COSINES[0], jnp.float32)
    sine = jnp.full((NTH, LANES), SINES[0], jnp.float32)
    for a in range(1, NTH):
        cosine = jnp.where(heading == a, COSINES[a], cosine)
        sine = jnp.where(heading == a, SINES[a], sine)
    for g in range(GROUPS):
        speed = SPEED_BASE + jnp.where(low_half, g, g + GROUPS).astype(jnp.float32) * SPEED_STEP
        table[0, :, lanes_of(g)] = cosine * speed * POS
        table[1, :, lanes_of(g)] = sine * speed * POS

    def split(vals):
        half = GROUPS // 2
        turned = [pltpu.roll(v, NW, 1) for v in vals]
        result = []
        for m in range(half):
            result.append(jnp.where(low_half, vals[m], turned[m + half]))
            result.append(jnp.where(low_half, turned[m], vals[m + half]))
        return result

    def joined(vals):
        half = GROUPS // 2
        turned = [pltpu.roll(v, NW, 1) for v in vals]
        return ([jnp.where(low_half, vals[2 * m], turned[2 * m + 1]) for m in range(half)]
                + [jnp.where(low_half, turned[2 * m], vals[2 * m + 1]) for m in range(half)])

    def row_slope(vals, tops):
        return tuple(
            functools.reduce(jnp.maximum, [jnp.abs(vals[g + 1] - vals[g]) for g in range(n, GROUPS - 1, len(tops))], top)
            for n, top in enumerate(tops))

    def seam_slope(step, tops):
        best = [zero, zero]
        for i in range(bx):
            for j in range(by):
                first = vb[step, i + 1, j + 1, :, lanes_of(0)]
                last = vb[step, i + 1, j + 1, :, lanes_of(GROUPS - 1)]
                best[j % 2] = jnp.maximum(best[j % 2], jnp.abs(pltpu.roll(first, NW, 1) - last))
        seam = jnp.where(low_half, jnp.maximum(best[0], best[1]), 0.0)
        return jnp.maximum(functools.reduce(jnp.maximum, tops), seam)

    for copy in loads:
        copy.wait()

    def first_rows(j, tops):
        rows = [split([nat_v[i, j, :, lanes_of(g)] for g in range(GROUPS)]) for i in range(bx)]
        for i, vals in enumerate(rows):
            for g in range(GROUPS):
                vb[0, i + 1, j + 1, :, lanes_of(g)] = vals[g]
            tops = row_slope(vals, tops)
        return tops

    top = seam_slope(0, lax.fori_loop(0, by, first_rows, (zero,) * 4))

    drift_copy.wait()
    east_ends = jnp.where(low_half, table[0, :, lanes_of(0)], table[0, :, lanes_of(GROUPS - 1)])
    north_ends = jnp.where(low_half, table[1, :, lanes_of(0)], table[1, :, lanes_of(GROUPS - 1)])
    best = [zero] * 2
    for i in range(bx):
        for j in range(by):
            both = jnp.abs(east_ends + drift[i, 0, j] * POS) + jnp.abs(north_ends + drift[i, 1, j] * POS)
            best[j % 2] = jnp.maximum(best[j % 2], both)
    rates[0] = jnp.max(jnp.maximum(best[0], best[1]))

    def split_obstacle(j, carry):
        for i in range(bx):
            vals = split([nat_o[i, j, :, lanes_of(g)] for g in range(GROUPS)])
            for g in range(GROUPS):
                ob[i, j, :, lanes_of(g)] = vals[g]
        return carry

    pl.semaphore_wait(ready, jnp.where(beside_exists, 1, 0) + len(plane) + len(column))

    def halo_copy(step, side):
        inner = {0: (1, pl.ds(1, by)), 1: (bx, pl.ds(1, by)), 2: (pl.ds(1, bx), 1), 3: (pl.ds(1, bx), by)}[side]
        outer = {0: (bx + 1, pl.ds(1, by)), 1: (0, pl.ds(1, by)), 2: (pl.ds(1, bx), by + 1), 3: (pl.ds(1, bx), 0)}[side]
        return pltpu.make_async_remote_copy(
            src_ref=vb.at[(step,) + inner], dst_ref=vb.at[(step,) + outer],
            send_sem=halo_send.at[step, side], recv_sem=halo_recv.at[step, side],
            device_id=sides[side][1], device_id_type=MESH)

    def ghost(step, side):
        if side < 2:
            to, near, far = ((0, 1, 2), (bx + 1, bx, bx - 1))[side]

            def fill(j, carry):
                vb[step, to, j] = 2.0 * vb[step, near, j] - vb[step, far, j]
                return carry

            lax.fori_loop(1, by + 1, fill, 0)
        else:
            to, near, far = ((0, 1, 2), (by + 1, by, by - 1))[side - 2]

            def fill(i, carry):
                vb[step, i, to] = 2.0 * vb[step, i, near] - vb[step, i, far]
                return carry

            lax.fori_loop(1, bx + 1, fill, 0)

    def spread(step, stage):
        for k, peer in enumerate(groups[stage]):
            pltpu.make_async_remote_copy(
                src_ref=sent.at[step, stage], dst_ref=got.at[step, stage, k],
                send_sem=max_send.at[step, stage], recv_sem=max_recv.at[step, stage],
                device_id=peer, device_id_type=MESH).start()

    def wait_all(step, stage, sem):
        pltpu.make_async_copy(got.at[step, stage], got.at[step, stage], sem.at[step, stage]).wait()

    def largest(step, stage, at):
        best = [sent[step, stage, at]] + [got[step, stage, k, at] for k in range(len(groups[stage]))]
        while len(best) > 1:
            best = [jnp.maximum(a, b) for a, b in zip(best[::2], best[1::2])] + best[len(best) // 2 * 2:]
        return best[0]

    def inner_terms(step):
        def row(i, j):
            vals = [vb[step, i, j, :, lanes_of(g)] for g in range(GROUPS)]
            seam_up = pltpu.roll(vals[0], NW, 1)
            seam_down = pltpu.roll(vals[GROUPS - 1], NW, 1)
            for g in range(GROUPS):
                v = vals[g]
                ahead = vals[g + 1] - v if g < GROUPS - 1 else seam_up - v
                behind = vals[g - 1] - v if g > 0 else seam_down - v
                if g == 0:
                    behind = jnp.where(low_half, -ahead, behind)
                if g == GROUPS - 1:
                    ahead = jnp.where(low_half, ahead, -behind)
                span = ahead - behind
                part_b[i - 1, j - 1, :, lanes_of(g)] = ahead + behind
                acc = span * span * (1.0 / (4.0 * SPEED_STEP * SPEED_STEP * 2.0 * EFFORT_COST * SCALE))
                right = pltpu.roll(v, LANES - 1, 1) - v
                left = pltpu.roll(v, 1, 1) - v
                acc += jnp.maximum(jnp.where(last_turn, -left, right), jnp.where(first_turn, -right, left))
                around = jnp.where(turn_up, pltpu.roll(v, NTH - 1, 0), pltpu.roll(v, 1, 0))
                acc += turn_w * (around - v)
                part_a[i - 1, j - 1, :, lanes_of(g)] = acc

        return row

    def position_terms(step):
        def row(i, j):
            dx = drift[i - 1, 0, j - 1] * POS
            dy = drift[i - 1, 1, j - 1] * POS
            for g in range(GROUPS):
                s = lanes_of(g)
                v = vb[step, i, j, :, s]
                east = table[0, :, s] + dx
                north = table[1, :, s] + dy
                from_x = jnp.where(east > 0.0, vb[step, i + 1, j, :, s], vb[step, i - 1, j, :, s])
                from_y = jnp.where(north > 0.0, vb[step, i, j + 1, :, s], vb[step, i, j - 1, :, s])
                part_a[i - 1, j - 1, :, s] += jnp.abs(east) * (from_x - v) + jnp.abs(north) * (from_y - v)

        return row

    def each(first, last, rows):
        def body(j, carry):
            rows(j)
            return carry

        lax.fori_loop(first, last, body, 0)

    def send_halos(step, two):
        for side in two:
            @pl.when(sides[side][0])
            def _(side=side):
                halo_copy(step, side).start()

    def take_halos(step, two):
        for side in two:
            @pl.when(jnp.logical_not(sides[side][0]))
            def _(side=side):
                ghost(step, side)

            @pl.when(sides[side][0])
            def _(side=side):
                halo_copy(step, opposite[side]).wait_recv()

    def share(step, top):
        inner, position = inner_terms(step), position_terms(step)
        sent[step, 0, 0] = jnp.max(top)
        sent[step, 0, 1] = rates[0]
        spread(step, 0)
        send_halos(step, (2, 3))

        def inner_rows(planes):
            def rows(j):
                for i in planes:
                    inner(i, j)

            return rows

        each(1, by + 1, inner_rows(range(1, bx // 2 + 1)))
        send_halos(step, (0, 1))
        each(1, by + 1, inner_rows(range(bx // 2 + 1, bx + 1)))
        wait_all(step, 0, max_recv)
        sent[step, 1, 0] = largest(step, 0, 0)

        @pl.when(step == 0)
        def _():
            rates[0] = largest(step, 0, 1)

        sent[step, 1, 1] = rates[0]
        spread(step, 1)

        @pl.when(step == 0)
        def _():
            ob_copy.wait()
            each(0, by, lambda j: split_obstacle(j, 0))

        take_halos(step, (2, 3))

        def middle(j):
            for i in range(2, bx):
                position(i, j)

        each(1, by + 1, middle)
        take_halos(step, (0, 1))

        def rims(j):
            for i in (1, bx):
                position(i, j)

        each(1, by + 1, rims)

    def weights(step):
        wait_all(step, 1, max_recv)
        slope = largest(step, 1, 0)

        @pl.when(step == 0)
        def _():
            rates[0] = largest(step, 1, 1)

        top_slope = jnp.full((NTH, LANES), slope, jnp.float32) * (1.0 / SPEED_STEP)
        rate_top = jnp.full((NTH, LANES), rates[0], jnp.float32) * SCALE + TURN_TOP + SCALE
        dt = COURANT / (rate_top + top_slope * (1.0 / (EFFORT_COST * SPEED_STEP)))
        times[step] = dt
        return SCALE * dt, dt * top_slope * (0.5 / (SPEED_STEP * EFFORT_COST))

    def one_step(step, top):
        share(step, top)
        weight_a, weight_b = weights(step)

        def update(j, tops):
            for i in range(bx):
                vals = []
                for g in range(GROUPS):
                    s = lanes_of(g)
                    moved = vb[step, i + 1, j + 1, :, s] + weight_a * part_a[i, j, :, s] + weight_b * part_b[i, j, :, s]
                    moved = jnp.minimum(moved, ob[i, j, :, s])
                    vb[step + 1, i + 1, j + 1, :, s] = moved
                    vals.append(moved)
                tops = row_slope(vals, tops)
            return tops

        tops = lax.fori_loop(0, by, update, (zero,) * 4)
        return seam_slope(step + 1, tops)

    top = lax.fori_loop(0, ITERS - 1, one_step, top)
    last = ITERS - 1
    share(last, top)

    weight_a, weight_b = weights(last)
    stores = []
    half = by // 2
    for i in range(bx):
        def final(part, carry, i=i):
            for n in range(half):
                j = part * half + n
                vals = []
                for g in range(GROUPS):
                    s = lanes_of(g)
                    vals.append(vb[last, i + 1, j + 1, :, s] + weight_a * part_a[i, j, :, s] + weight_b * part_b[i, j, :, s])
                for g, moved in enumerate(joined(vals)):
                    ob[i, j, :, lanes_of(g)] = jnp.minimum(moved, nat_o[i, j, :, lanes_of(g)])
            return carry

        lax.fori_loop(0, 2, final, 0)
        copy = pltpu.make_async_copy(ob.at[i], out_hbm.at[i], out_sem.at[i])
        copy.start()
        stores.append(copy)

    for step in range(ITERS):
        steps_out[step] = jnp.max(times[step])

    def finish(step, carry):
        for stage in range(2):
            wait_all(step, stage, max_send)
        for side in range(4):
            @pl.when(sides[side][0])
            def _(side=side):
                halo_copy(step, side).wait_send()
        return carry

    lax.fori_loop(0, ITERS, finish, 0)
    for copy in stores:
        copy.wait()


def per_device(nx, ny, value_field, obstacle, drift_field):
    bx, by = value_field.shape[:2]
    shape = value_field.shape
    hbm = pl.BlockSpec(memory_space=pltpu.MemorySpace.HBM)
    dma = pltpu.SemaphoreType.DMA
    block = pltpu.VMEM(shape, jnp.float32)
    return pl.pallas_call(
        functools.partial(kernel, nx, ny, bx, by),
        out_shape=(jax.ShapeDtypeStruct(shape, jnp.float32), jax.ShapeDtypeStruct((ITERS,), jnp.float32)),
        in_specs=[hbm, hbm, hbm],
        out_specs=(pl.BlockSpec(memory_space=pl.ANY), pl.BlockSpec(memory_space=pltpu.SMEM)),
        scratch_shapes=[
            pltpu.VMEM((ITERS, bx + 2, by + 2) + shape[2:], jnp.float32),
            block, block, block, block, block,
            pltpu.VMEM((2,) + shape[2:], jnp.float32),
            pltpu.SMEM((bx, 2, by), jnp.float32),
            pltpu.SMEM((ITERS, 2, 8), jnp.float32),
            pltpu.SMEM((ITERS, 2, len(PLANE), 8), jnp.float32),
            pltpu.SMEM((1,), jnp.float32),
            pltpu.VMEM((ITERS, NTH, LANES), jnp.float32),
            dma((bx,)), dma, dma, dma((bx,)),
            dma((ITERS, 4)), dma((ITERS, 4)), dma((ITERS, 2)), dma((ITERS, 2)),
        ],
        compiler_params=pltpu.CompilerParams(
            collective_id=0, has_side_effects=True, vmem_limit_bytes=52 * 1024 * 1024),
        name="safe_set_steps",
    )(jnp.transpose(drift_field, (0, 2, 1)), value_field, obstacle)


def solution(mesh):
    nx, ny = mesh.shape["gx"], mesh.shape["gy"]
    placed = (P("gx", "gy", None, None), P("gx", "gy", None, None), P("gx", "gy", None))
    return jax.shard_map(
        functools.partial(per_device, nx, ny),
        mesh=mesh,
        in_specs=placed,
        out_specs=(P("gx", "gy", None, None), P()),
        check_vma=False,
    )
```

```python
import functools
import math

import jax
import jax.numpy as jnp
import numpy as np
from jax import lax
from jax.experimental import pallas as pl
from jax.experimental.pallas import tpu as pltpu
from jax.sharding import PartitionSpec as P

NTH = 8
NV = 16
NW = 64
ITERS = 4
SPACE_STEP = 0.5
SPEED_BASE = 1.0
SPEED_STEP = 0.2
TURN_LIMIT = 0.25
EFFORT_COST = 10.0
COURANT = 0.9

LANES = 128
GROUPS = NV * NW // LANES
CHIP_X = 4
CHIP_Y = 4
CORES = 2
MESH = pl.DeviceIdType.MESH

HEAD_STEP = 2.0 * math.pi / NTH
TURN_STEP = 2.0 / NW
SCALE = TURN_LIMIT / TURN_STEP
POS = 1.0 / (SPACE_STEP * SCALE)

F32 = np.float32
HEADINGS = (np.arange(NTH, dtype=F32) * F32(HEAD_STEP)).astype(np.float64)
COSINES = [float(F32(c)) for c in np.cos(HEADINGS)]
SINES = [float(F32(s)) for s in np.sin(HEADINGS)]
TURN_TOP = float(F32((1.0 - 1.0 / NW)) / F32(HEAD_STEP))

PLANE = sorted(((a, b) for a in range(CHIP_Y) for b in range(CHIP_X)),
               key=lambda t: -(min(t[0], CHIP_Y - t[0]) + min(t[1], CHIP_X - t[1])))


def lanes_of(g):
    return slice(g * LANES, (g + 1) * LANES)


def kernel(nx, ny, bx, by,
           drift_hbm, value_hbm, barrier_hbm, out_hbm, steps_out,
           vb, nat_v, nat_o, ob, part_a, part_b, table, drift, pair, sent, got, rates, times, held,
           in_sem, ob_sem, drift_sem, out_sem, halo_send, halo_recv,
           pair_send, pair_recv, max_send, max_recv):
    me_x = lax.axis_index("gx")
    me_y = lax.axis_index("gy")
    chip = me_x // CORES
    core = lax.rem(me_x, CORES)
    chip_y = chip // CHIP_X
    chip_x = lax.rem(chip, CHIP_X)
    partner = (chip * CORES + 1 - core, me_y)
    plane = [(lax.rem(chip_y + a, CHIP_Y) * CHIP_X + lax.rem(chip_x + b, CHIP_X)) * CORES + core for a, b in PLANE]
    others = ny * len(PLANE) - 1
    low_x, high_x = me_x > 0, me_x < nx - 1
    low_y, high_y = me_y > 0, me_y < ny - 1
    sides = ((low_x, (me_x - 1, me_y)), (high_x, (me_x + 1, me_y)),
             (low_y, (me_x, me_y - 1)), (high_y, (me_x, me_y + 1)))
    opposite = (1, 0, 3, 2)
    def layer(k):
        half = (k + 1) // 2
        return lax.rem(me_y + ny // 2 + half * (2 * lax.rem(k, 2) - 1) + ny, ny)

    def for_others(act):
        def body(k, carry):
            z = layer(k)
            for n, gx in enumerate(plane):
                run = functools.partial(act, k * len(plane) + n, (gx, z))
                if n == len(plane) - 1:
                    pl.when(k < ny - 1)(run)
                else:
                    run()
            return carry

        lax.fori_loop(0, ny, body, 0)

    loads = []
    for i in range(bx):
        copy = pltpu.make_async_copy(value_hbm.at[i], nat_v.at[i], in_sem.at[i])
        copy.start()
        loads.append(copy)
    drift_copy = pltpu.make_async_copy(drift_hbm, drift, drift_sem)
    drift_copy.start()
    ob_copy = pltpu.make_async_copy(barrier_hbm, nat_o, ob_sem)
    ob_copy.start()

    ready = pltpu.get_barrier_semaphore()

    def greet(n, peer):
        pl.semaphore_signal(ready, inc=1, device_id=peer, device_id_type=MESH)

    for_others(greet)
    greet(0, partner)
    beside_exists = jnp.where(core == 0, me_x - 1 >= 0, me_x + 1 < nx)
    beside = me_x - 1 + 2 * core

    @pl.when(beside_exists)
    def _():
        pl.semaphore_signal(ready, inc=1, device_id=(beside, me_y), device_id_type=MESH)

    lane = lax.broadcasted_iota(jnp.int32, (NTH, LANES), 1)
    low_half = lane < NW
    in_row = lax.rem(lane, NW)
    first_turn = in_row == 0
    last_turn = in_row == NW - 1
    turn_up = in_row >= NW // 2
    turning = -1.0 + (in_row.astype(jnp.float32) + 0.5) * (2.0 / NW)
    turn_w = jnp.abs(turning) * (1.0 / (HEAD_STEP * SCALE))
    zero = jnp.zeros((NTH, LANES), jnp.float32)

    heading = lax.broadcasted_iota(jnp.int32, (NTH, LANES), 0)
    cosine = jnp.full((NTH, LANES), COSINES[0], jnp.float32)
    sine = jnp.full((NTH, LANES), SINES[0], jnp.float32)
    for a in range(1, NTH):
        cosine = jnp.where(heading == a, COSINES[a], cosine)
        sine = jnp.where(heading == a, SINES[a], sine)
    for g in range(GROUPS):
        speed = SPEED_BASE + jnp.where(low_half, g, g + GROUPS).astype(jnp.float32) * SPEED_STEP
        table[0, :, lanes_of(g)] = cosine * speed * POS
        table[1, :, lanes_of(g)] = sine * speed * POS

    def split(vals):
        half = GROUPS // 2
        turned = [pltpu.roll(v, NW, 1) for v in vals]
        result = []
        for m in range(half):
            result.append(jnp.where(low_half, vals[m], turned[m + half]))
            result.append(jnp.where(low_half, turned[m], vals[m + half]))
        return result

    def joined(vals):
        half = GROUPS // 2
        turned = [pltpu.roll(v, NW, 1) for v in vals]
        return ([jnp.where(low_half, vals[2 * m], turned[2 * m + 1]) for m in range(half)]
                + [jnp.where(low_half, turned[2 * m], vals[2 * m + 1]) for m in range(half)])

    def row_slope(vals, tops):
        return tuple(
            functools.reduce(jnp.maximum, [jnp.abs(vals[g + 1] - vals[g]) for g in range(n, GROUPS - 1, len(tops))], top)
            for n, top in enumerate(tops))

    def seam_slope(step, tops):
        best = [zero, zero]
        for i in range(bx):
            for j in range(by):
                first = vb[step, i + 1, j + 1, :, lanes_of(0)]
                last = vb[step, i + 1, j + 1, :, lanes_of(GROUPS - 1)]
                best[j % 2] = jnp.maximum(best[j % 2], jnp.abs(pltpu.roll(first, NW, 1) - last))
        seam = jnp.where(low_half, jnp.maximum(best[0], best[1]), 0.0)
        return jnp.maximum(functools.reduce(jnp.maximum, tops), seam)

    for copy in loads:
        copy.wait()

    def first_rows(j, tops):
        rows = [split([nat_v[i, j, :, lanes_of(g)] for g in range(GROUPS)]) for i in range(bx)]
        for i, vals in enumerate(rows):
            for g in range(GROUPS):
                vb[0, i + 1, j + 1, :, lanes_of(g)] = vals[g]
            tops = row_slope(vals, tops)
        return tops

    top = seam_slope(0, lax.fori_loop(0, by, first_rows, (zero,) * 4))

    drift_copy.wait()
    east_ends = jnp.where(low_half, table[0, :, lanes_of(0)], table[0, :, lanes_of(GROUPS - 1)])
    north_ends = jnp.where(low_half, table[1, :, lanes_of(0)], table[1, :, lanes_of(GROUPS - 1)])
    best = [zero] * 2
    for i in range(bx):
        for j in range(by):
            both = jnp.abs(east_ends + drift[i, 0, j] * POS) + jnp.abs(north_ends + drift[i, 1, j] * POS)
            best[j % 2] = jnp.maximum(best[j % 2], both)
    rates[0] = jnp.max(jnp.maximum(best[0], best[1]))

    def split_obstacle(j, carry):
        for i in range(bx):
            vals = split([nat_o[i, j, :, lanes_of(g)] for g in range(GROUPS)])
            for g in range(GROUPS):
                ob[i + 1, j + 1, :, lanes_of(g)] = vals[g]
        return carry

    pl.semaphore_wait(ready, jnp.where(beside_exists, 1, 0) + others + 1)

    def rim_copy(ref, at, side):
        inner = {0: (1, pl.ds(1, by)), 1: (bx, pl.ds(1, by)), 2: (pl.ds(1, bx), 1), 3: (pl.ds(1, bx), by)}[side]
        outer = {0: (bx + 1, pl.ds(1, by)), 1: (0, pl.ds(1, by)), 2: (pl.ds(1, bx), by + 1), 3: (pl.ds(1, bx), 0)}[side]
        return pltpu.make_async_remote_copy(
            src_ref=ref.at[inner], dst_ref=ref.at[outer],
            send_sem=halo_send.at[at, side], recv_sem=halo_recv.at[at, side],
            device_id=sides[side][1], device_id_type=MESH)

    def send_rims(ref, at):
        for side in (2, 3, 0, 1):
            @pl.when(sides[side][0])
            def _(side=side):
                rim_copy(ref, at, side).start()

    def take_rims(ref, at):
        for side in range(4):
            @pl.when(sides[side][0])
            def _(side=side):
                rim_copy(ref, at, opposite[side]).wait_recv()

    def ghost(step, side):
        if side < 2:
            to, near, far = ((0, 1, 2), (bx + 1, bx, bx - 1))[side]

            def fill(j, carry):
                vb[step, to, j] = 2.0 * vb[step, near, j] - vb[step, far, j]
                return carry

            lax.fori_loop(1, by + 1, fill, 0)
        else:
            to, near, far = ((0, 1, 2), (by + 1, by, by - 1))[side - 2]

            def fill(i, carry):
                vb[step, i, to] = 2.0 * vb[step, i, near] - vb[step, i, far]
                return carry

            lax.fori_loop(1, bx + 1, fill, 0)

    def pair_copy(step):
        return pltpu.make_async_remote_copy(
            src_ref=pair.at[step, 0], dst_ref=pair.at[step, 1],
            send_sem=pair_send.at[step], recv_sem=pair_recv.at[step],
            device_id=partner, device_id_type=MESH)

    def spread(step):
        def send(n, peer):
            pltpu.make_async_remote_copy(
                src_ref=sent.at[step], dst_ref=got.at[step, n],
                send_sem=max_send.at[step], recv_sem=max_recv.at[step],
                device_id=peer, device_id_type=MESH).start()

        for_others(send)

    def wait_all(step, sem):
        rows = got.at[step, pl.ds(0, others)]
        pltpu.make_async_copy(rows, rows, sem.at[step]).wait()

    def largest(step, at):
        best = [sent[step, at]] + [got[step, n, at] for n in range(3)]
        for n in range(3, others):
            best[n % 4] = jnp.maximum(best[n % 4], got[step, n, at])
        return jnp.maximum(jnp.maximum(best[0], best[1]), jnp.maximum(best[2], best[3]))

    def speed_sides(vals):
        seam_up = pltpu.roll(vals[0], NW, 1)
        seam_down = pltpu.roll(vals[GROUPS - 1], NW, 1)
        result = []
        for g, v in enumerate(vals):
            ahead = vals[g + 1] - v if g < GROUPS - 1 else seam_up - v
            behind = vals[g - 1] - v if g > 0 else seam_down - v
            if g == 0:
                behind = jnp.where(low_half, -ahead, behind)
            if g == GROUPS - 1:
                ahead = jnp.where(low_half, ahead, -behind)
            result.append((ahead, behind))
        return result

    def inner_terms(step):
        def row(i, j):
            vals = [vb[step, i, j, :, lanes_of(g)] for g in range(GROUPS)]
            for g, (ahead, behind) in enumerate(speed_sides(vals)):
                v = vals[g]
                span = ahead - behind
                part_b[i - 1, j - 1, :, lanes_of(g)] = ahead + behind
                acc = span * span * (1.0 / (4.0 * SPEED_STEP * SPEED_STEP * 2.0 * EFFORT_COST * SCALE))
                right = pltpu.roll(v, LANES - 1, 1) - v
                left = pltpu.roll(v, 1, 1) - v
                acc += jnp.maximum(jnp.where(last_turn, -left, right), jnp.where(first_turn, -right, left))
                around = jnp.where(turn_up, pltpu.roll(v, NTH - 1, 0), pltpu.roll(v, 1, 0))
                acc += turn_w * (around - v)
                part_a[step, i, j, :, lanes_of(g)] = acc

        return row

    def position_terms(step):
        def row(i, j):
            dx = drift[i - 1, 0, j - 1] * POS
            dy = drift[i - 1, 1, j - 1] * POS
            for g in range(GROUPS):
                s = lanes_of(g)
                v = vb[step, i, j, :, s]
                east = table[0, :, s] + dx
                north = table[1, :, s] + dy
                from_x = jnp.where(east > 0.0, vb[step, i + 1, j, :, s], vb[step, i - 1, j, :, s])
                from_y = jnp.where(north > 0.0, vb[step, i, j + 1, :, s], vb[step, i, j - 1, :, s])
                part_a[step, i, j, :, s] += jnp.abs(east) * (from_x - v) + jnp.abs(north) * (from_y - v)

        return row

    def each(first, last, rows):
        def body(j, carry):
            rows(j)
            return carry

        lax.fori_loop(first, last, body, 0)

    def halo_row(step, i, j):
        before = step - 1
        vals = [vb[before, i, j, :, lanes_of(g)] for g in range(GROUPS)]
        for g, (ahead, behind) in enumerate(speed_sides(vals)):
            s = lanes_of(g)
            moved = vals[g] + held[0] * part_a[before, i, j, :, s] + held[1] * (ahead + behind)
            vb[step, i, j, :, s] = jnp.minimum(moved, ob[i, j, :, s])

    def halo_rows(step):
        for side, i in ((0, 0), (1, bx + 1)):
            @pl.when(sides[side][0])
            def _(i=i):
                def pair_of_rows(n):
                    halo_row(step, i, 2 * n + 1)
                    halo_row(step, i, 2 * n + 2)

                each(0, by // 2, pair_of_rows)

        for side, j in ((2, 0), (3, by + 1)):
            @pl.when(sides[side][0])
            def _(j=j):
                def pair_of_rows(n):
                    halo_row(step, 2 * n + 1, j)
                    halo_row(step, 2 * n + 2, j)

                each(0, bx // 2, pair_of_rows)

    def share(step, top):
        inner, position = inner_terms(step), position_terms(step)
        pair[step, 0, 0] = jnp.max(top)
        pair[step, 0, 1] = rates[0]
        pair_copy(step).start()

        def inner_rows(planes):
            def rows(j):
                for i in planes:
                    inner(i, j)

            return rows

        each(1, 2, inner_rows(range(1, bx + 1)))
        pair_copy(step).wait_recv()
        sent[step, 0] = jnp.maximum(pair[step, 0, 0], pair[step, 1, 0])
        sent[step, 1] = jnp.maximum(pair[step, 0, 1], pair[step, 1, 1])
        spread(step)

        @pl.when(step == 0)
        def _():
            send_rims(vb.at[0], 0)

        each(2, by + 1, inner_rows(range(1, bx + 1)))

        @pl.when(step == 0)
        def _():
            ob_copy.wait()
            each(0, by, lambda j: split_obstacle(j, 0))
            send_rims(ob, ITERS)
            take_rims(vb.at[0], 0)

        @pl.when(step == 1)
        def _():
            take_rims(ob, ITERS)

        @pl.when(step > 0)
        def _():
            take_rims(part_a.at[step - 1], step)
            halo_rows(step)

        for side in range(4):
            @pl.when(jnp.logical_not(sides[side][0]))
            def _(side=side):
                ghost(step, side)

        def x_rims(j):
            position(1, j)
            position(bx, j)

        def y_rims(i):
            position(i, 1)
            position(i, by)

        def inside(j):
            for i in range(2, bx):
                position(i, j)

        each(1, by + 1, x_rims)
        each(2, bx, y_rims)

        @pl.when(step < ITERS - 1)
        def _():
            send_rims(part_a.at[step], step + 1)

        each(2, by, inside)

    def weights(step):
        wait_all(step, max_recv)
        slope = largest(step, 0)

        @pl.when(step == 0)
        def _():
            rates[0] = largest(step, 1)

        top_slope = jnp.full((NTH, LANES), slope, jnp.float32) * (1.0 / SPEED_STEP)
        rate_top = jnp.full((NTH, LANES), rates[0], jnp.float32) * SCALE + TURN_TOP + SCALE
        dt = COURANT / (rate_top + top_slope * (1.0 / (EFFORT_COST * SPEED_STEP)))
        times[step] = dt
        held[0] = SCALE * dt
        held[1] = dt * top_slope * (0.5 / (SPEED_STEP * EFFORT_COST))
        return held[0], held[1]

    def one_step(step, top):
        share(step, top)
        weight_a, weight_b = weights(step)

        def update(j, tops):
            for i in range(1, bx + 1):
                vals = []
                for g in range(GROUPS):
                    s = lanes_of(g)
                    moved = vb[step, i, j, :, s] + weight_a * part_a[step, i, j, :, s] + weight_b * part_b[i - 1, j - 1, :, s]
                    moved = jnp.minimum(moved, ob[i, j, :, s])
                    vb[step + 1, i, j, :, s] = moved
                    vals.append(moved)
                tops = row_slope(vals, tops)
            return tops

        tops = lax.fori_loop(1, by + 1, update, (zero,) * 4)
        return seam_slope(step + 1, tops)

    top = lax.fori_loop(0, ITERS - 1, one_step, top)
    last = ITERS - 1
    share(last, top)

    weight_a, weight_b = weights(last)
    stores = []
    half = by // 2
    for i in range(bx):
        def final(part, carry, i=i):
            for n in range(half):
                j = part * half + n
                vals = []
                for g in range(GROUPS):
                    s = lanes_of(g)
                    vals.append(vb[last, i + 1, j + 1, :, s] + weight_a * part_a[last, i + 1, j + 1, :, s]
                                + weight_b * part_b[i, j, :, s])
                for g, moved in enumerate(joined(vals)):
                    nat_v[i, j, :, lanes_of(g)] = jnp.minimum(moved, nat_o[i, j, :, lanes_of(g)])
            return carry

        lax.fori_loop(0, 2, final, 0)
        copy = pltpu.make_async_copy(nat_v.at[i], out_hbm.at[i], out_sem.at[i])
        copy.start()
        stores.append(copy)

    for step in range(ITERS):
        steps_out[step] = jnp.max(times[step])

    def finish(step, carry):
        pair_copy(step).wait_send()
        wait_all(step, max_send)
        return carry

    lax.fori_loop(0, ITERS, finish, 0)

    def rims_sent(at, carry):
        for side in range(4):
            @pl.when(sides[side][0])
            def _(side=side):
                rim_copy(ob, at, side).wait_send()
        return carry

    lax.fori_loop(0, ITERS + 1, rims_sent, 0)
    for copy in stores:
        copy.wait()


def per_device(nx, ny, value_field, obstacle, drift_field):
    bx, by = value_field.shape[:2]
    shape = value_field.shape
    hbm = pl.BlockSpec(memory_space=pltpu.MemorySpace.HBM)
    dma = pltpu.SemaphoreType.DMA
    block = pltpu.VMEM(shape, jnp.float32)
    return pl.pallas_call(
        functools.partial(kernel, nx, ny, bx, by),
        out_shape=(jax.ShapeDtypeStruct(shape, jnp.float32), jax.ShapeDtypeStruct((ITERS,), jnp.float32)),
        in_specs=[hbm, hbm, hbm],
        out_specs=(pl.BlockSpec(memory_space=pl.ANY), pl.BlockSpec(memory_space=pltpu.SMEM)),
        scratch_shapes=[
            pltpu.VMEM((ITERS, bx + 2, by + 2) + shape[2:], jnp.float32),
            block, block,
            pltpu.VMEM((bx + 2, by + 2) + shape[2:], jnp.float32),
            pltpu.VMEM((ITERS, bx + 2, by + 2) + shape[2:], jnp.float32),
            block,
            pltpu.VMEM((2,) + shape[2:], jnp.float32),
            pltpu.SMEM((bx, 2, by), jnp.float32),
            pltpu.SMEM((ITERS, 2, 8), jnp.float32),
            pltpu.SMEM((ITERS, 8), jnp.float32),
            pltpu.SMEM((ITERS, ny * len(PLANE) - 1, 8), jnp.float32),
            pltpu.SMEM((1,), jnp.float32),
            pltpu.VMEM((ITERS, NTH, LANES), jnp.float32),
            pltpu.VMEM((2, NTH, LANES), jnp.float32),
            dma((bx,)), dma, dma, dma((bx,)),
            dma((ITERS + 1, 4)), dma((ITERS + 1, 4)), dma((ITERS,)), dma((ITERS,)), dma((ITERS,)), dma((ITERS,)),
        ],
        compiler_params=pltpu.CompilerParams(
            collective_id=0, has_side_effects=True, vmem_limit_bytes=52 * 1024 * 1024),
        name="safe_set_steps",
    )(jnp.transpose(drift_field, (0, 2, 1)), value_field, obstacle)


def solution(mesh):
    nx, ny = mesh.shape["gx"], mesh.shape["gy"]
    placed = (P("gx", "gy", None, None), P("gx", "gy", None, None), P("gx", "gy", None))
    return jax.shard_map(
        functools.partial(per_device, nx, ny),
        mesh=mesh,
        in_specs=placed,
        out_specs=(P("gx", "gy", None, None), P()),
        check_vma=False,
    )
```

```python
import functools
import math

import jax
import jax.numpy as jnp
import numpy as np
from jax import lax
from jax.experimental import pallas as pl
from jax.experimental.pallas import tpu as pltpu
from jax.sharding import PartitionSpec as P

NTH = 8
NV = 16
NW = 64
ITERS = 4
SPACE_STEP = 0.5
SPEED_BASE = 1.0
SPEED_STEP = 0.2
TURN_LIMIT = 0.25
EFFORT_COST = 10.0
COURANT = 0.9

LANES = 128
GROUPS = NV * NW // LANES
CHIP_X = 4
CHIP_Y = 4
CORES = 2
MESH = pl.DeviceIdType.MESH

HEAD_STEP = 2.0 * math.pi / NTH
TURN_STEP = 2.0 / NW
SCALE = TURN_LIMIT / TURN_STEP
POS = 1.0 / (SPACE_STEP * SCALE)

F32 = np.float32
HEADINGS = (np.arange(NTH, dtype=F32) * F32(HEAD_STEP)).astype(np.float64)
COSINES = [float(F32(c)) for c in np.cos(HEADINGS)]
SINES = [float(F32(s)) for s in np.sin(HEADINGS)]
TURN_TOP = float(F32((1.0 - 1.0 / NW)) / F32(HEAD_STEP))

PLANE = sorted(((a, b) for a in range(CHIP_Y) for b in range(CHIP_X)),
               key=lambda t: -(min(t[0], CHIP_Y - t[0]) + min(t[1], CHIP_X - t[1])))


def lanes_of(g):
    return slice(g * LANES, (g + 1) * LANES)


def kernel(nx, ny, bx, by,
           drift_hbm, value_hbm, barrier_hbm, out_hbm, steps_out,
           vb, nat_v, nat_o, ob, part_a, part_b, table, drift, pair, sent, got, rates, times, held,
           in_sem, ob_sem, drift_sem, out_sem, halo_send, halo_recv,
           pair_send, pair_recv, max_send, max_recv):
    me_x = lax.axis_index("gx")
    me_y = lax.axis_index("gy")
    chip = me_x // CORES
    core = lax.rem(me_x, CORES)
    chip_y = chip // CHIP_X
    chip_x = lax.rem(chip, CHIP_X)
    partner = (chip * CORES + 1 - core, me_y)
    plane = [(lax.rem(chip_y + a, CHIP_Y) * CHIP_X + lax.rem(chip_x + b, CHIP_X)) * CORES + core for a, b in PLANE]
    others = ny * len(PLANE) - 1
    low_x, high_x = me_x > 0, me_x < nx - 1
    low_y, high_y = me_y > 0, me_y < ny - 1
    sides = ((low_x, (me_x - 1, me_y)), (high_x, (me_x + 1, me_y)),
             (low_y, (me_x, me_y - 1)), (high_y, (me_x, me_y + 1)))
    opposite = (1, 0, 3, 2)
    def layer(k):
        half = (k + 1) // 2
        return lax.rem(me_y + ny // 2 + half * (2 * lax.rem(k, 2) - 1) + ny, ny)

    def for_others(act):
        def body(k, carry):
            z = layer(k)
            for n, gx in enumerate(plane):
                run = functools.partial(act, k * len(plane) + n, (gx, z))
                if n == len(plane) - 1:
                    pl.when(k < ny - 1)(run)
                else:
                    run()
            return carry

        lax.fori_loop(0, ny, body, 0)

    loads = []
    for i in range(bx):
        copy = pltpu.make_async_copy(value_hbm.at[i], nat_v.at[i], in_sem.at[i])
        copy.start()
        loads.append(copy)
    drift_copy = pltpu.make_async_copy(drift_hbm, drift, drift_sem)
    drift_copy.start()
    ob_copy = pltpu.make_async_copy(barrier_hbm, nat_o, ob_sem)
    ob_copy.start()

    ready = pltpu.get_barrier_semaphore()

    def greet(n, peer):
        pl.semaphore_signal(ready, inc=1, device_id=peer, device_id_type=MESH)

    for_others(greet)
    greet(0, partner)
    beside_exists = jnp.where(core == 0, me_x - 1 >= 0, me_x + 1 < nx)
    beside = me_x - 1 + 2 * core

    @pl.when(beside_exists)
    def _():
        pl.semaphore_signal(ready, inc=1, device_id=(beside, me_y), device_id_type=MESH)

    lane = lax.broadcasted_iota(jnp.int32, (NTH, LANES), 1)
    low_half = lane < NW
    in_row = lax.rem(lane, NW)
    first_turn = in_row == 0
    last_turn = in_row == NW - 1
    turn_up = in_row >= NW // 2
    turning = -1.0 + (in_row.astype(jnp.float32) + 0.5) * (2.0 / NW)
    turn_w = jnp.abs(turning) * (1.0 / (HEAD_STEP * SCALE))
    zero = jnp.zeros((NTH, LANES), jnp.float32)

    heading = lax.broadcasted_iota(jnp.int32, (NTH, LANES), 0)
    cosine = jnp.full((NTH, LANES), COSINES[0], jnp.float32)
    sine = jnp.full((NTH, LANES), SINES[0], jnp.float32)
    for a in range(1, NTH):
        cosine = jnp.where(heading == a, COSINES[a], cosine)
        sine = jnp.where(heading == a, SINES[a], sine)
    for g in range(GROUPS):
        speed = SPEED_BASE + jnp.where(low_half, g, g + GROUPS).astype(jnp.float32) * SPEED_STEP
        table[0, :, lanes_of(g)] = cosine * speed * POS
        table[1, :, lanes_of(g)] = sine * speed * POS

    def split(vals):
        half = GROUPS // 2
        turned = [pltpu.roll(v, NW, 1) for v in vals]
        result = []
        for m in range(half):
            result.append(jnp.where(low_half, vals[m], turned[m + half]))
            result.append(jnp.where(low_half, turned[m], vals[m + half]))
        return result

    def joined(vals):
        half = GROUPS // 2
        turned = [pltpu.roll(v, NW, 1) for v in vals]
        return ([jnp.where(low_half, vals[2 * m], turned[2 * m + 1]) for m in range(half)]
                + [jnp.where(low_half, turned[2 * m], vals[2 * m + 1]) for m in range(half)])

    def row_slope(vals, tops):
        return tuple(
            functools.reduce(jnp.maximum, [jnp.abs(vals[g + 1] - vals[g]) for g in range(n, GROUPS - 1, len(tops))], top)
            for n, top in enumerate(tops))

    def seam_slope(step, tops):
        best = [zero, zero]
        for i in range(bx):
            for j in range(by):
                first = vb[step, i + 1, j + 1, :, lanes_of(0)]
                last = vb[step, i + 1, j + 1, :, lanes_of(GROUPS - 1)]
                best[j % 2] = jnp.maximum(best[j % 2], jnp.abs(pltpu.roll(first, NW, 1) - last))
        seam = jnp.where(low_half, jnp.maximum(best[0], best[1]), 0.0)
        return jnp.maximum(functools.reduce(jnp.maximum, tops), seam)

    for copy in loads:
        copy.wait()

    def first_rows(j, tops):
        rows = [split([nat_v[i, j, :, lanes_of(g)] for g in range(GROUPS)]) for i in range(bx)]
        for i, vals in enumerate(rows):
            for g in range(GROUPS):
                vb[0, i + 1, j + 1, :, lanes_of(g)] = vals[g]
            tops = row_slope(vals, tops)
        return tops

    top = seam_slope(0, lax.fori_loop(0, by, first_rows, (zero,) * 4))

    drift_copy.wait()
    east_ends = jnp.where(low_half, table[0, :, lanes_of(0)], table[0, :, lanes_of(GROUPS - 1)])
    north_ends = jnp.where(low_half, table[1, :, lanes_of(0)], table[1, :, lanes_of(GROUPS - 1)])
    best = [zero] * 2
    for i in range(bx):
        for j in range(by):
            both = jnp.abs(east_ends + drift[i, 0, j] * POS) + jnp.abs(north_ends + drift[i, 1, j] * POS)
            best[j % 2] = jnp.maximum(best[j % 2], both)
    rates[0] = jnp.max(jnp.maximum(best[0], best[1]))

    def split_obstacle(j, carry):
        for i in range(bx):
            vals = split([nat_o[i, j, :, lanes_of(g)] for g in range(GROUPS)])
            for g in range(GROUPS):
                ob[i + 1, j + 1, :, lanes_of(g)] = vals[g]
        return carry

    pl.semaphore_wait(ready, jnp.where(beside_exists, 1, 0) + others + 1)

    def rim_copy(ref, at, side):
        inner = {0: (1, pl.ds(1, by)), 1: (bx, pl.ds(1, by)), 2: (pl.ds(1, bx), 1), 3: (pl.ds(1, bx), by)}[side]
        outer = {0: (bx + 1, pl.ds(1, by)), 1: (0, pl.ds(1, by)), 2: (pl.ds(1, bx), by + 1), 3: (pl.ds(1, bx), 0)}[side]
        return pltpu.make_async_remote_copy(
            src_ref=ref.at[inner], dst_ref=ref.at[outer],
            send_sem=halo_send.at[at, side], recv_sem=halo_recv.at[at, side],
            device_id=sides[side][1], device_id_type=MESH)

    def send_rims(ref, at):
        for side in (2, 3, 0, 1):
            @pl.when(sides[side][0])
            def _(side=side):
                rim_copy(ref, at, side).start()

    def take_rims(ref, at):
        for side in range(4):
            @pl.when(sides[side][0])
            def _(side=side):
                rim_copy(ref, at, opposite[side]).wait_recv()

    def ghost(step, side):
        if side < 2:
            to, near, far = ((0, 1, 2), (bx + 1, bx, bx - 1))[side]

            def fill(j, carry):
                vb[step, to, j] = 2.0 * vb[step, near, j] - vb[step, far, j]
                return carry

            lax.fori_loop(1, by + 1, fill, 0)
        else:
            to, near, far = ((0, 1, 2), (by + 1, by, by - 1))[side - 2]

            def fill(i, carry):
                vb[step, i, to] = 2.0 * vb[step, i, near] - vb[step, i, far]
                return carry

            lax.fori_loop(1, bx + 1, fill, 0)

    send_rims(vb.at[0], 0)

    def pair_copy(step):
        return pltpu.make_async_remote_copy(
            src_ref=pair.at[step, 0], dst_ref=pair.at[step, 1],
            send_sem=pair_send.at[step], recv_sem=pair_recv.at[step],
            device_id=partner, device_id_type=MESH)

    def spread(step):
        def send(n, peer):
            pltpu.make_async_remote_copy(
                src_ref=sent.at[step], dst_ref=got.at[step, n],
                send_sem=max_send.at[step], recv_sem=max_recv.at[step],
                device_id=peer, device_id_type=MESH).start()

        for_others(send)

    def wait_all(step, sem):
        rows = got.at[step, pl.ds(0, others)]
        pltpu.make_async_copy(rows, rows, sem.at[step]).wait()

    def largest(step, at):
        best = [sent[step, at]] + [got[step, n, at] for n in range(3)]
        for n in range(3, others):
            best[n % 4] = jnp.maximum(best[n % 4], got[step, n, at])
        return jnp.maximum(jnp.maximum(best[0], best[1]), jnp.maximum(best[2], best[3]))

    def speed_sides(vals):
        seam_up = pltpu.roll(vals[0], NW, 1)
        seam_down = pltpu.roll(vals[GROUPS - 1], NW, 1)
        result = []
        for g, v in enumerate(vals):
            ahead = vals[g + 1] - v if g < GROUPS - 1 else seam_up - v
            behind = vals[g - 1] - v if g > 0 else seam_down - v
            if g == 0:
                behind = jnp.where(low_half, -ahead, behind)
            if g == GROUPS - 1:
                ahead = jnp.where(low_half, ahead, -behind)
            result.append((ahead, behind))
        return result

    def inner_terms(step):
        def row(i, j):
            vals = [vb[step, i, j, :, lanes_of(g)] for g in range(GROUPS)]
            for g, (ahead, behind) in enumerate(speed_sides(vals)):
                v = vals[g]
                span = ahead - behind
                part_b[i - 1, j - 1, :, lanes_of(g)] = ahead + behind
                acc = span * span * (1.0 / (4.0 * SPEED_STEP * SPEED_STEP * 2.0 * EFFORT_COST * SCALE))
                right = pltpu.roll(v, LANES - 1, 1) - v
                left = pltpu.roll(v, 1, 1) - v
                acc += jnp.maximum(jnp.where(last_turn, -left, right), jnp.where(first_turn, -right, left))
                around = jnp.where(turn_up, pltpu.roll(v, NTH - 1, 0), pltpu.roll(v, 1, 0))
                acc += turn_w * (around - v)
                part_a[step, i, j, :, lanes_of(g)] = acc

        return row

    def position_terms(step):
        def row(i, j):
            dx = drift[i - 1, 0, j - 1] * POS
            dy = drift[i - 1, 1, j - 1] * POS
            for g in range(GROUPS):
                s = lanes_of(g)
                v = vb[step, i, j, :, s]
                east = table[0, :, s] + dx
                north = table[1, :, s] + dy
                from_x = jnp.where(east > 0.0, vb[step, i + 1, j, :, s], vb[step, i - 1, j, :, s])
                from_y = jnp.where(north > 0.0, vb[step, i, j + 1, :, s], vb[step, i, j - 1, :, s])
                part_a[step, i, j, :, s] += jnp.abs(east) * (from_x - v) + jnp.abs(north) * (from_y - v)

        return row

    def each(first, last, rows):
        def body(j, carry):
            rows(j)
            return carry

        lax.fori_loop(first, last, body, 0)

    def halo_row(step, i, j):
        before = step - 1
        vals = [vb[before, i, j, :, lanes_of(g)] for g in range(GROUPS)]
        for g, (ahead, behind) in enumerate(speed_sides(vals)):
            s = lanes_of(g)
            moved = vals[g] + held[0] * part_a[before, i, j, :, s] + held[1] * (ahead + behind)
            vb[step, i, j, :, s] = jnp.minimum(moved, ob[i, j, :, s])

    def halo_rows(step):
        for side, i in ((0, 0), (1, bx + 1)):
            @pl.when(sides[side][0])
            def _(i=i):
                def pair_of_rows(n):
                    halo_row(step, i, 2 * n + 1)
                    halo_row(step, i, 2 * n + 2)

                each(0, by // 2, pair_of_rows)

        for side, j in ((2, 0), (3, by + 1)):
            @pl.when(sides[side][0])
            def _(j=j):
                def pair_of_rows(n):
                    halo_row(step, 2 * n + 1, j)
                    halo_row(step, 2 * n + 2, j)

                each(0, bx // 2, pair_of_rows)

    def share(step, top):
        inner, position = inner_terms(step), position_terms(step)
        pair[step, 0, 0] = jnp.max(top)
        pair[step, 0, 1] = rates[0]
        pair_copy(step).start()

        def inner_rows(planes):
            def rows(j):
                for i in planes:
                    inner(i, j)

            return rows

        def y_rim_rows(n):
            for i in range(1, bx + 1):
                inner(i, n * (by - 1) + 1)

        def x_rim_rows(j):
            inner(1, j)
            inner(bx, j)

        each(0, 2, y_rim_rows)
        each(2, 4, x_rim_rows)
        pair_copy(step).wait_recv()
        sent[step, 0] = jnp.maximum(pair[step, 0, 0], pair[step, 1, 0])
        sent[step, 1] = jnp.maximum(pair[step, 0, 1], pair[step, 1, 1])
        spread(step)

        each(4, by, x_rim_rows)

        @pl.when(step == 0)
        def _():
            ob_copy.wait()
            each(0, by, lambda j: split_obstacle(j, 0))
            send_rims(ob, ITERS)
            take_rims(vb.at[0], 0)

        @pl.when(step == 1)
        def _():
            take_rims(ob, ITERS)

        @pl.when(step > 0)
        def _():
            take_rims(part_a.at[step - 1], step)
            halo_rows(step)

        for side in range(4):
            @pl.when(jnp.logical_not(sides[side][0]))
            def _(side=side):
                ghost(step, side)

        def x_rims(j):
            position(1, j)
            position(bx, j)

        def y_rims(i):
            position(i, 1)
            position(i, by)

        def inside(j):
            for i in range(2, bx):
                position(i, j)

        each(1, by + 1, x_rims)
        each(2, bx, y_rims)

        @pl.when(step < ITERS - 1)
        def _():
            send_rims(part_a.at[step], step + 1)

        each(2, by, inner_rows(range(2, bx)))
        each(2, by, inside)

    def weights(step):
        wait_all(step, max_recv)
        slope = largest(step, 0)

        @pl.when(step == 0)
        def _():
            rates[0] = largest(step, 1)

        top_slope = jnp.full((NTH, LANES), slope, jnp.float32) * (1.0 / SPEED_STEP)
        rate_top = jnp.full((NTH, LANES), rates[0], jnp.float32) * SCALE + TURN_TOP + SCALE
        dt = COURANT / (rate_top + top_slope * (1.0 / (EFFORT_COST * SPEED_STEP)))
        times[step] = dt
        held[0] = SCALE * dt
        held[1] = dt * top_slope * (0.5 / (SPEED_STEP * EFFORT_COST))
        return held[0], held[1]

    def one_step(step, top):
        share(step, top)
        weight_a, weight_b = weights(step)

        def update(n, tops):
            for i, j in [(i, 2 * n + m) for m in (1, 2) for i in range(1, bx + 1)]:
                vals = []
                for g in range(GROUPS):
                    s = lanes_of(g)
                    moved = vb[step, i, j, :, s] + weight_a * part_a[step, i, j, :, s] + weight_b * part_b[i - 1, j - 1, :, s]
                    moved = jnp.minimum(moved, ob[i, j, :, s])
                    vb[step + 1, i, j, :, s] = moved
                    vals.append(moved)
                tops = row_slope(vals, tops)
            return tops

        tops = lax.fori_loop(0, by // 2, update, (zero,) * 4)
        return seam_slope(step + 1, tops)

    top = lax.fori_loop(0, ITERS - 1, one_step, top)
    last = ITERS - 1
    share(last, top)

    weight_a, weight_b = weights(last)
    stores = []
    half = by // 2
    for i in range(bx):
        def final(part, carry, i=i):
            for n in range(half):
                j = part * half + n
                vals = []
                for g in range(GROUPS):
                    s = lanes_of(g)
                    vals.append(vb[last, i + 1, j + 1, :, s] + weight_a * part_a[last, i + 1, j + 1, :, s]
                                + weight_b * part_b[i, j, :, s])
                for g, moved in enumerate(joined(vals)):
                    nat_v[i, j, :, lanes_of(g)] = jnp.minimum(moved, nat_o[i, j, :, lanes_of(g)])
            return carry

        lax.fori_loop(0, 2, final, 0)
        copy = pltpu.make_async_copy(nat_v.at[i], out_hbm.at[i], out_sem.at[i])
        copy.start()
        stores.append(copy)

    for step in range(ITERS):
        steps_out[step] = jnp.max(times[step])

    def finish(step, carry):
        pair_copy(step).wait_send()
        wait_all(step, max_send)
        return carry

    lax.fori_loop(0, ITERS, finish, 0)

    def rims_sent(at, carry):
        for side in range(4):
            @pl.when(sides[side][0])
            def _(side=side):
                rim_copy(ob, at, side).wait_send()
        return carry

    lax.fori_loop(0, ITERS + 1, rims_sent, 0)
    for copy in stores:
        copy.wait()


def per_device(nx, ny, value_field, obstacle, drift_field):
    bx, by = value_field.shape[:2]
    shape = value_field.shape
    hbm = pl.BlockSpec(memory_space=pltpu.MemorySpace.HBM)
    dma = pltpu.SemaphoreType.DMA
    block = pltpu.VMEM(shape, jnp.float32)
    return pl.pallas_call(
        functools.partial(kernel, nx, ny, bx, by),
        out_shape=(jax.ShapeDtypeStruct(shape, jnp.float32), jax.ShapeDtypeStruct((ITERS,), jnp.float32)),
        in_specs=[hbm, hbm, hbm],
        out_specs=(pl.BlockSpec(memory_space=pl.ANY), pl.BlockSpec(memory_space=pltpu.SMEM)),
        scratch_shapes=[
            pltpu.VMEM((ITERS, bx + 2, by + 2) + shape[2:], jnp.float32),
            block, block,
            pltpu.VMEM((bx + 2, by + 2) + shape[2:], jnp.float32),
            pltpu.VMEM((ITERS, bx + 2, by + 2) + shape[2:], jnp.float32),
            block,
            pltpu.VMEM((2,) + shape[2:], jnp.float32),
            pltpu.SMEM((bx, 2, by), jnp.float32),
            pltpu.SMEM((ITERS, 2, 8), jnp.float32),
            pltpu.SMEM((ITERS, 8), jnp.float32),
            pltpu.SMEM((ITERS, ny * len(PLANE) - 1, 8), jnp.float32),
            pltpu.SMEM((1,), jnp.float32),
            pltpu.VMEM((ITERS, NTH, LANES), jnp.float32),
            pltpu.VMEM((2, NTH, LANES), jnp.float32),
            dma((bx,)), dma, dma, dma((bx,)),
            dma((ITERS + 1, 4)), dma((ITERS + 1, 4)), dma((ITERS,)), dma((ITERS,)), dma((ITERS,)), dma((ITERS,)),
        ],
        compiler_params=pltpu.CompilerParams(
            collective_id=0, has_side_effects=True, vmem_limit_bytes=52 * 1024 * 1024),
        name="safe_set_steps",
    )(pltpu.with_memory_space_constraint(jnp.transpose(drift_field, (0, 2, 1)), pltpu.MemorySpace.HBM), value_field, obstacle)


def solution(mesh):
    nx, ny = mesh.shape["gx"], mesh.shape["gy"]
    placed = (P("gx", "gy", None, None), P("gx", "gy", None, None), P("gx", "gy", None))
    return jax.shard_map(
        functools.partial(per_device, nx, ny),
        mesh=mesh,
        in_specs=placed,
        out_specs=(P("gx", "gy", None, None), P()),
        check_vma=False,
    )
```

```python
import functools
import math

import jax
import jax.numpy as jnp
import numpy as np
from jax import lax
from jax.experimental import pallas as pl
from jax.experimental.pallas import tpu as pltpu
from jax.sharding import PartitionSpec as P

NTH = 8
NV = 16
NW = 64
ITERS = 4
SPACE_STEP = 0.5
SPEED_BASE = 1.0
SPEED_STEP = 0.2
TURN_LIMIT = 0.25
EFFORT_COST = 10.0
COURANT = 0.9

LANES = 128
GROUPS = NV * NW // LANES
CHIP_X = 4
CHIP_Y = 4
CORES = 2
MESH = pl.DeviceIdType.MESH

HEAD_STEP = 2.0 * math.pi / NTH
TURN_STEP = 2.0 / NW
SCALE = TURN_LIMIT / TURN_STEP
POS = 1.0 / (SPACE_STEP * SCALE)

F32 = np.float32
HEADINGS = (np.arange(NTH, dtype=F32) * F32(HEAD_STEP)).astype(np.float64)
COSINES = [float(F32(c)) for c in np.cos(HEADINGS)]
SINES = [float(F32(s)) for s in np.sin(HEADINGS)]
TURN_TOP = float(F32((1.0 - 1.0 / NW)) / F32(HEAD_STEP))

PLANE = sorted(((a, b) for a in range(CHIP_Y) for b in range(CHIP_X)),
               key=lambda t: -(min(t[0], CHIP_Y - t[0]) + min(t[1], CHIP_X - t[1])))


def lanes_of(g):
    return slice(g * LANES, (g + 1) * LANES)


def kernel(nx, ny, bx, by,
           drift_hbm, value_hbm, barrier_hbm, out_hbm, steps_out,
           vb, nat_v, nat_o, ob, part_a, part_b, table, drift, pair, sent, got, rates, local_rate, times, held,
           in_sem, ob_sem, drift_sem, out_sem, halo_send, halo_recv,
           pair_send, pair_recv, max_send, max_recv):
    me_x = lax.axis_index("gx")
    me_y = lax.axis_index("gy")
    chip = me_x // CORES
    core = lax.rem(me_x, CORES)
    chip_y = chip // CHIP_X
    chip_x = lax.rem(chip, CHIP_X)
    partner = (chip * CORES + 1 - core, me_y)
    plane = [(lax.rem(chip_y + a, CHIP_Y) * CHIP_X + lax.rem(chip_x + b, CHIP_X)) * CORES + core for a, b in PLANE]
    others = ny * len(PLANE) - 1
    low_x, high_x = me_x > 0, me_x < nx - 1
    low_y, high_y = me_y > 0, me_y < ny - 1
    sides = ((low_x, (me_x - 1, me_y)), (high_x, (me_x + 1, me_y)),
             (low_y, (me_x, me_y - 1)), (high_y, (me_x, me_y + 1)))
    opposite = (1, 0, 3, 2)
    def layer(k):
        half = (k + 1) // 2
        return lax.rem(me_y + ny // 2 + half * (2 * lax.rem(k, 2) - 1) + ny, ny)

    def for_others(act):
        def body(k, carry):
            z = layer(k)
            for n, gx in enumerate(plane):
                run = functools.partial(act, k * len(plane) + n, (gx, z))
                if n == len(plane) - 1:
                    pl.when(k < ny - 1)(run)
                else:
                    run()
            return carry

        lax.fori_loop(0, ny, body, 0)

    loads = []
    for i in range(bx):
        copy = pltpu.make_async_copy(value_hbm.at[i], nat_v.at[i], in_sem.at[i])
        copy.start()
        loads.append(copy)
    drift_copy = pltpu.make_async_copy(drift_hbm, drift, drift_sem)
    drift_copy.start()
    ob_copy = pltpu.make_async_copy(barrier_hbm, nat_o, ob_sem)
    ob_copy.start()

    ready = pltpu.get_barrier_semaphore()

    def greet(n, peer):
        pl.semaphore_signal(ready, inc=1, device_id=peer, device_id_type=MESH)

    for_others(greet)
    greet(0, partner)
    beside_exists = jnp.where(core == 0, me_x - 1 >= 0, me_x + 1 < nx)
    beside = me_x - 1 + 2 * core

    @pl.when(beside_exists)
    def _():
        pl.semaphore_signal(ready, inc=1, device_id=(beside, me_y), device_id_type=MESH)

    lane = lax.broadcasted_iota(jnp.int32, (NTH, LANES), 1)
    low_half = lane < NW
    in_row = lax.rem(lane, NW)
    first_turn = in_row == 0
    last_turn = in_row == NW - 1
    turn_up = in_row >= NW // 2
    turning = -1.0 + (in_row.astype(jnp.float32) + 0.5) * (2.0 / NW)
    turn_w = jnp.abs(turning) * (1.0 / (HEAD_STEP * SCALE))
    zero = jnp.zeros((NTH, LANES), jnp.float32)

    heading = lax.broadcasted_iota(jnp.int32, (NTH, LANES), 0)
    cosine = jnp.full((NTH, LANES), COSINES[0], jnp.float32)
    sine = jnp.full((NTH, LANES), SINES[0], jnp.float32)
    for a in range(1, NTH):
        cosine = jnp.where(heading == a, COSINES[a], cosine)
        sine = jnp.where(heading == a, SINES[a], sine)
    for g in range(GROUPS):
        speed = SPEED_BASE + jnp.where(low_half, g, g + GROUPS).astype(jnp.float32) * SPEED_STEP
        table[0, :, lanes_of(g)] = cosine * speed * POS
        table[1, :, lanes_of(g)] = sine * speed * POS

    def split(vals):
        half = GROUPS // 2
        turned = [pltpu.roll(v, NW, 1) for v in vals]
        result = []
        for m in range(half):
            result.append(jnp.where(low_half, vals[m], turned[m + half]))
            result.append(jnp.where(low_half, turned[m], vals[m + half]))
        return result

    def joined(vals):
        half = GROUPS // 2
        turned = [pltpu.roll(v, NW, 1) for v in vals]
        return ([jnp.where(low_half, vals[2 * m], turned[2 * m + 1]) for m in range(half)]
                + [jnp.where(low_half, turned[2 * m], vals[2 * m + 1]) for m in range(half)])

    def row_slope(vals, tops):
        return tuple(
            functools.reduce(jnp.maximum, [jnp.abs(vals[g + 1] - vals[g]) for g in range(n, GROUPS - 1, len(tops))], top)
            for n, top in enumerate(tops))

    def seam_slope(step, tops):
        best = [zero, zero]
        for i in range(bx):
            for j in range(by):
                first = vb[step, i + 1, j + 1, :, lanes_of(0)]
                last = vb[step, i + 1, j + 1, :, lanes_of(GROUPS - 1)]
                best[j % 2] = jnp.maximum(best[j % 2], jnp.abs(pltpu.roll(first, NW, 1) - last))
        seam = jnp.where(low_half, jnp.maximum(best[0], best[1]), 0.0)
        return jnp.maximum(functools.reduce(jnp.maximum, tops), seam)

    for copy in loads:
        copy.wait()

    def first_rows(j, tops):
        rows = [split([nat_v[i, j, :, lanes_of(g)] for g in range(GROUPS)]) for i in range(bx)]
        for i, vals in enumerate(rows):
            for g in range(GROUPS):
                vb[0, i + 1, j + 1, :, lanes_of(g)] = vals[g]
            tops = row_slope(vals, tops)
        return tops

    top = seam_slope(0, lax.fori_loop(0, by, first_rows, (zero,) * 4))

    drift_copy.wait()
    east_ends = jnp.where(low_half, table[0, :, lanes_of(0)], table[0, :, lanes_of(GROUPS - 1)])
    north_ends = jnp.where(low_half, table[1, :, lanes_of(0)], table[1, :, lanes_of(GROUPS - 1)])
    best = [zero] * 2
    for i in range(bx):
        for j in range(by):
            both = jnp.abs(east_ends + drift[i, 0, j] * POS) + jnp.abs(north_ends + drift[i, 1, j] * POS)
            best[j % 2] = jnp.maximum(best[j % 2], both)
    local_rate[...] = jnp.maximum(best[0], best[1])

    def split_obstacle(j, carry):
        for i in range(bx):
            vals = split([nat_o[i, j, :, lanes_of(g)] for g in range(GROUPS)])
            for g in range(GROUPS):
                ob[i + 1, j + 1, :, lanes_of(g)] = vals[g]
        return carry

    pl.semaphore_wait(ready, jnp.where(beside_exists, 1, 0) + others + 1)

    def rim_copy(ref, at, side):
        inner = {0: (1, pl.ds(1, by)), 1: (bx, pl.ds(1, by)), 2: (pl.ds(1, bx), 1), 3: (pl.ds(1, bx), by)}[side]
        outer = {0: (bx + 1, pl.ds(1, by)), 1: (0, pl.ds(1, by)), 2: (pl.ds(1, bx), by + 1), 3: (pl.ds(1, bx), 0)}[side]
        return pltpu.make_async_remote_copy(
            src_ref=ref.at[inner], dst_ref=ref.at[outer],
            send_sem=halo_send.at[at, side], recv_sem=halo_recv.at[at, side],
            device_id=sides[side][1], device_id_type=MESH)

    def send_rims(ref, at):
        for side in (2, 3, 0, 1):
            @pl.when(sides[side][0])
            def _(side=side):
                rim_copy(ref, at, side).start()

    def take_rims(ref, at):
        for side in range(4):
            @pl.when(sides[side][0])
            def _(side=side):
                rim_copy(ref, at, opposite[side]).wait_recv()

    def ghost(step, side):
        if side < 2:
            to, near, far = ((0, 1, 2), (bx + 1, bx, bx - 1))[side]

            def fill(j, carry):
                vb[step, to, j] = 2.0 * vb[step, near, j] - vb[step, far, j]
                return carry

            lax.fori_loop(1, by + 1, fill, 0)
        else:
            to, near, far = ((0, 1, 2), (by + 1, by, by - 1))[side - 2]

            def fill(i, carry):
                vb[step, i, to] = 2.0 * vb[step, i, near] - vb[step, i, far]
                return carry

            lax.fori_loop(1, bx + 1, fill, 0)

    send_rims(vb.at[0], 0)

    def pair_copy(step):
        return pltpu.make_async_remote_copy(
            src_ref=pair.at[step, 0], dst_ref=pair.at[step, 1],
            send_sem=pair_send.at[step], recv_sem=pair_recv.at[step],
            device_id=partner, device_id_type=MESH)

    def spread(step):
        def send(n, peer):
            pltpu.make_async_remote_copy(
                src_ref=sent.at[step], dst_ref=got.at[step, n],
                send_sem=max_send.at[step], recv_sem=max_recv.at[step],
                device_id=peer, device_id_type=MESH).start()

        for_others(send)

    def wait_all(step, sem):
        rows = got.at[step, pl.ds(0, others)]
        pltpu.make_async_copy(rows, rows, sem.at[step]).wait()

    def largest(step, at):
        best = [sent[step, at]] + [got[step, n, at] for n in range(7)]
        for n in range(7, others):
            best[n % 8] = jnp.maximum(best[n % 8], got[step, n, at])
        return functools.reduce(jnp.maximum, best)

    def speed_sides(vals):
        seam_up = pltpu.roll(vals[0], NW, 1)
        seam_down = pltpu.roll(vals[GROUPS - 1], NW, 1)
        result = []
        for g, v in enumerate(vals):
            ahead = vals[g + 1] - v if g < GROUPS - 1 else seam_up - v
            behind = vals[g - 1] - v if g > 0 else seam_down - v
            if g == 0:
                behind = jnp.where(low_half, -ahead, behind)
            if g == GROUPS - 1:
                ahead = jnp.where(low_half, ahead, -behind)
            result.append((ahead, behind))
        return result

    def inner_terms(step):
        def row(i, j):
            vals = [vb[step, i, j, :, lanes_of(g)] for g in range(GROUPS)]
            for g, (ahead, behind) in enumerate(speed_sides(vals)):
                v = vals[g]
                span = ahead - behind
                part_b[i - 1, j - 1, :, lanes_of(g)] = ahead + behind
                acc = span * span * (1.0 / (4.0 * SPEED_STEP * SPEED_STEP * 2.0 * EFFORT_COST * SCALE))
                right = pltpu.roll(v, LANES - 1, 1) - v
                left = pltpu.roll(v, 1, 1) - v
                acc += jnp.maximum(jnp.where(last_turn, -left, right), jnp.where(first_turn, -right, left))
                around = jnp.where(turn_up, pltpu.roll(v, NTH - 1, 0), pltpu.roll(v, 1, 0))
                acc += turn_w * (around - v)
                part_a[step, i, j, :, lanes_of(g)] = acc

        return row

    def position_terms(step):
        def row(i, j):
            dx = drift[i - 1, 0, j - 1] * POS
            dy = drift[i - 1, 1, j - 1] * POS
            for g in range(GROUPS):
                s = lanes_of(g)
                v = vb[step, i, j, :, s]
                east = table[0, :, s] + dx
                north = table[1, :, s] + dy
                from_x = jnp.where(east > 0.0, vb[step, i + 1, j, :, s], vb[step, i - 1, j, :, s])
                from_y = jnp.where(north > 0.0, vb[step, i, j + 1, :, s], vb[step, i, j - 1, :, s])
                part_a[step, i, j, :, s] += jnp.abs(east) * (from_x - v) + jnp.abs(north) * (from_y - v)

        return row

    def each(first, last, rows):
        def body(j, carry):
            rows(j)
            return carry

        lax.fori_loop(first, last, body, 0)

    def halo_row(step, i, j):
        before = step - 1
        vals = [vb[before, i, j, :, lanes_of(g)] for g in range(GROUPS)]
        for g, (ahead, behind) in enumerate(speed_sides(vals)):
            s = lanes_of(g)
            moved = vals[g] + held[0] * part_a[before, i, j, :, s] + held[1] * (ahead + behind)
            vb[step, i, j, :, s] = jnp.minimum(moved, ob[i, j, :, s])

    def halo_rows(step):
        for side, i in ((0, 0), (1, bx + 1)):
            @pl.when(sides[side][0])
            def _(i=i):
                def pair_of_rows(n):
                    halo_row(step, i, 2 * n + 1)
                    halo_row(step, i, 2 * n + 2)

                each(0, by // 2, pair_of_rows)

        for side, j in ((2, 0), (3, by + 1)):
            @pl.when(sides[side][0])
            def _(j=j):
                def pair_of_rows(n):
                    halo_row(step, 2 * n + 1, j)
                    halo_row(step, 2 * n + 2, j)

                each(0, bx // 2, pair_of_rows)

    def share(step, top):
        inner, position = inner_terms(step), position_terms(step)
        pair[step, 0, 0] = top
        pair[step, 0, 1] = local_rate[...]
        pair_copy(step).start()

        def inner_rows(planes):
            def rows(j):
                for i in planes:
                    inner(i, j)

            return rows

        def y_rim_rows(n):
            for i in range(1, bx + 1):
                inner(i, n * (by - 1) + 1)

        def x_rim_rows(j):
            inner(1, j)
            inner(bx, j)

        each(0, 2, y_rim_rows)
        each(2, 4, x_rim_rows)
        pair_copy(step).wait_recv()
        sent[step, 0] = jnp.max(jnp.maximum(pair[step, 0, 0], pair[step, 1, 0]))

        @pl.when(step == 0)
        def _():
            rates[0] = jnp.max(jnp.maximum(pair[step, 0, 1], pair[step, 1, 1]))

        sent[step, 1] = rates[0]
        spread(step)

        each(4, by, x_rim_rows)

        @pl.when(step == 0)
        def _():
            ob_copy.wait()
            each(0, by, lambda j: split_obstacle(j, 0))
            send_rims(ob, ITERS)
            take_rims(vb.at[0], 0)

        @pl.when(step == 1)
        def _():
            take_rims(ob, ITERS)

        @pl.when(step > 0)
        def _():
            take_rims(part_a.at[step - 1], step)
            halo_rows(step)

        for side in range(4):
            @pl.when(jnp.logical_not(sides[side][0]))
            def _(side=side):
                ghost(step, side)

        def x_rims(j):
            position(1, j)
            position(bx, j)

        def y_rims(i):
            position(i, 1)
            position(i, by)

        def inside(j):
            for i in range(2, bx):
                position(i, j)

        each(1, by + 1, x_rims)
        each(2, bx, y_rims)

        @pl.when(step < ITERS - 1)
        def _():
            send_rims(part_a.at[step], step + 1)

        each(2, by, inner_rows(range(2, bx)))
        each(2, by, inside)

    def weights(step):
        wait_all(step, max_recv)
        slope = largest(step, 0)

        @pl.when(step == 0)
        def _():
            rates[0] = largest(step, 1)

        top_slope = jnp.full((NTH, LANES), slope, jnp.float32) * (1.0 / SPEED_STEP)
        rate_top = jnp.full((NTH, LANES), rates[0], jnp.float32) * SCALE + TURN_TOP + SCALE
        dt = COURANT / (rate_top + top_slope * (1.0 / (EFFORT_COST * SPEED_STEP)))
        times[step] = dt
        held[0] = SCALE * dt
        held[1] = dt * top_slope * (0.5 / (SPEED_STEP * EFFORT_COST))
        return held[0], held[1]

    def one_step(step, top):
        share(step, top)
        weight_a, weight_b = weights(step)

        def update(n, tops):
            for i, j in [(i, 2 * n + m) for m in (1, 2) for i in range(1, bx + 1)]:
                vals = []
                for g in range(GROUPS):
                    s = lanes_of(g)
                    moved = vb[step, i, j, :, s] + weight_a * part_a[step, i, j, :, s] + weight_b * part_b[i - 1, j - 1, :, s]
                    moved = jnp.minimum(moved, ob[i, j, :, s])
                    vb[step + 1, i, j, :, s] = moved
                    vals.append(moved)
                tops = row_slope(vals, tops)
            return tops

        tops = lax.fori_loop(0, by // 2, update, (zero,) * 4)
        return seam_slope(step + 1, tops)

    top = lax.fori_loop(0, ITERS - 1, one_step, top)
    last = ITERS - 1
    share(last, top)

    weight_a, weight_b = weights(last)
    stores = []
    half = by // 2
    for i in range(bx):
        def final(part, carry, i=i):
            for n in range(half):
                j = part * half + n
                vals = []
                for g in range(GROUPS):
                    s = lanes_of(g)
                    vals.append(vb[last, i + 1, j + 1, :, s] + weight_a * part_a[last, i + 1, j + 1, :, s]
                                + weight_b * part_b[i, j, :, s])
                for g, moved in enumerate(joined(vals)):
                    nat_v[i, j, :, lanes_of(g)] = jnp.minimum(moved, nat_o[i, j, :, lanes_of(g)])
            return carry

        lax.fori_loop(0, 2, final, 0)
        copy = pltpu.make_async_copy(nat_v.at[i], out_hbm.at[i], out_sem.at[i])
        copy.start()
        stores.append(copy)

    for step in range(ITERS):
        steps_out[step] = jnp.max(times[step])

    def finish(step, carry):
        pair_copy(step).wait_send()
        wait_all(step, max_send)
        return carry

    lax.fori_loop(0, ITERS, finish, 0)

    def rims_sent(at, carry):
        for side in range(4):
            @pl.when(sides[side][0])
            def _(side=side):
                rim_copy(ob, at, side).wait_send()
        return carry

    lax.fori_loop(0, ITERS + 1, rims_sent, 0)
    for copy in stores:
        copy.wait()


def per_device(nx, ny, value_field, obstacle, drift_field):
    bx, by = value_field.shape[:2]
    shape = value_field.shape
    hbm = pl.BlockSpec(memory_space=pltpu.MemorySpace.HBM)
    dma = pltpu.SemaphoreType.DMA
    block = pltpu.VMEM(shape, jnp.float32)
    return pl.pallas_call(
        functools.partial(kernel, nx, ny, bx, by),
        out_shape=(jax.ShapeDtypeStruct(shape, jnp.float32), jax.ShapeDtypeStruct((ITERS,), jnp.float32)),
        in_specs=[hbm, hbm, hbm],
        out_specs=(pl.BlockSpec(memory_space=pl.ANY), pl.BlockSpec(memory_space=pltpu.SMEM)),
        scratch_shapes=[
            pltpu.VMEM((ITERS, bx + 2, by + 2) + shape[2:], jnp.float32),
            block, block,
            pltpu.VMEM((bx + 2, by + 2) + shape[2:], jnp.float32),
            pltpu.VMEM((ITERS, bx + 2, by + 2) + shape[2:], jnp.float32),
            block,
            pltpu.VMEM((2,) + shape[2:], jnp.float32),
            pltpu.SMEM((bx, 2, by), jnp.float32),
            pltpu.VMEM((ITERS, 2, 2, NTH, LANES), jnp.float32),
            pltpu.SMEM((ITERS, 8), jnp.float32),
            pltpu.SMEM((ITERS, ny * len(PLANE) - 1, 8), jnp.float32),
            pltpu.SMEM((1,), jnp.float32),
            pltpu.VMEM((NTH, LANES), jnp.float32),
            pltpu.VMEM((ITERS, NTH, LANES), jnp.float32),
            pltpu.VMEM((2, NTH, LANES), jnp.float32),
            dma((bx,)), dma, dma, dma((bx,)),
            dma((ITERS + 1, 4)), dma((ITERS + 1, 4)), dma((ITERS,)), dma((ITERS,)), dma((ITERS,)), dma((ITERS,)),
        ],
        compiler_params=pltpu.CompilerParams(
            collective_id=0, has_side_effects=True, vmem_limit_bytes=52 * 1024 * 1024),
        name="safe_set_steps",
    )(pltpu.with_memory_space_constraint(jnp.transpose(drift_field, (0, 2, 1)), pltpu.MemorySpace.HBM), value_field, obstacle)


def solution(mesh):
    nx, ny = mesh.shape["gx"], mesh.shape["gy"]
    placed = (P("gx", "gy", None, None), P("gx", "gy", None, None), P("gx", "gy", None))
    return jax.shard_map(
        functools.partial(per_device, nx, ny),
        mesh=mesh,
        in_specs=placed,
        out_specs=(P("gx", "gy", None, None), P()),
        check_vma=False,
    )
```

```python
import functools
import math

import jax
import jax.numpy as jnp
import numpy as np
from jax import lax
from jax.experimental import pallas as pl
from jax.experimental.pallas import tpu as pltpu
from jax.sharding import PartitionSpec as P

NTH = 8
NV = 16
NW = 64
ITERS = 4
SPACE_STEP = 0.5
SPEED_BASE = 1.0
SPEED_STEP = 0.2
TURN_LIMIT = 0.25
EFFORT_COST = 10.0
COURANT = 0.9

LANES = 128
GROUPS = NV * NW // LANES
CHIP_X = 4
CHIP_Y = 4
CORES = 2
MESH = pl.DeviceIdType.MESH

HEAD_STEP = 2.0 * math.pi / NTH
TURN_STEP = 2.0 / NW
SCALE = TURN_LIMIT / TURN_STEP
POS = 1.0 / (SPACE_STEP * SCALE)

F32 = np.float32
HEADINGS = (np.arange(NTH, dtype=F32) * F32(HEAD_STEP)).astype(np.float64)
COSINES = [float(F32(c)) for c in np.cos(HEADINGS)]
SINES = [float(F32(s)) for s in np.sin(HEADINGS)]
TURN_TOP = float(F32((1.0 - 1.0 / NW)) / F32(HEAD_STEP))

PLANE = sorted(((a, b) for a in range(CHIP_Y) for b in range(CHIP_X)),
               key=lambda t: -(min(t[0], CHIP_Y - t[0]) + min(t[1], CHIP_X - t[1])))


def lanes_of(g):
    return slice(g * LANES, (g + 1) * LANES)


def kernel(nx, ny, bx, by,
           drift_hbm, value_hbm, barrier_hbm, out_hbm, steps_out,
           vb, nat_v, nat_o, ob, part_a, part_b, table, drift, pair, sent, got, rates, local_rate, times, held,
           in_sem, ob_sem, drift_sem, out_sem, halo_send, halo_recv,
           pair_send, pair_recv, max_send, max_recv):
    me_x = lax.axis_index("gx")
    me_y = lax.axis_index("gy")
    chip = me_x // CORES
    core = lax.rem(me_x, CORES)
    chip_y = chip // CHIP_X
    chip_x = lax.rem(chip, CHIP_X)
    partner = (chip * CORES + 1 - core, me_y)
    plane = [(lax.rem(chip_y + a, CHIP_Y) * CHIP_X + lax.rem(chip_x + b, CHIP_X)) * CORES + core for a, b in PLANE]
    others = ny * len(PLANE) - 1
    low_x, high_x = me_x > 0, me_x < nx - 1
    low_y, high_y = me_y > 0, me_y < ny - 1
    sides = ((low_x, (me_x - 1, me_y)), (high_x, (me_x + 1, me_y)),
             (low_y, (me_x, me_y - 1)), (high_y, (me_x, me_y + 1)))
    opposite = (1, 0, 3, 2)
    def layer(k):
        half = (k + 1) // 2
        return lax.rem(me_y + ny // 2 + half * (2 * lax.rem(k, 2) - 1) + ny, ny)

    def for_others(act):
        def body(k, carry):
            z = layer(k)
            for n, gx in enumerate(plane):
                run = functools.partial(act, k * len(plane) + n, (gx, z))
                if n == len(plane) - 1:
                    pl.when(k < ny - 1)(run)
                else:
                    run()
            return carry

        lax.fori_loop(0, ny, body, 0)

    loads = []
    for i in range(bx):
        copy = pltpu.make_async_copy(value_hbm.at[i], nat_v.at[i], in_sem.at[i])
        copy.start()
        loads.append(copy)
    drift_copy = pltpu.make_async_copy(drift_hbm, drift, drift_sem)
    drift_copy.start()
    ob_copy = pltpu.make_async_copy(barrier_hbm, nat_o, ob_sem)
    ob_copy.start()

    ready = pltpu.get_barrier_semaphore()

    def greet(n, peer):
        pl.semaphore_signal(ready, inc=1, device_id=peer, device_id_type=MESH)

    for_others(greet)
    greet(0, partner)
    beside_exists = jnp.where(core == 0, me_x - 1 >= 0, me_x + 1 < nx)
    beside = me_x - 1 + 2 * core

    @pl.when(beside_exists)
    def _():
        pl.semaphore_signal(ready, inc=1, device_id=(beside, me_y), device_id_type=MESH)

    lane = lax.broadcasted_iota(jnp.int32, (NTH, LANES), 1)
    low_half = lane < NW
    in_row = lax.rem(lane, NW)
    first_turn = in_row == 0
    last_turn = in_row == NW - 1
    turn_up = in_row >= NW // 2
    turning = -1.0 + (in_row.astype(jnp.float32) + 0.5) * (2.0 / NW)
    turn_w = jnp.abs(turning) * (1.0 / (HEAD_STEP * SCALE))
    zero = jnp.zeros((NTH, LANES), jnp.float32)

    heading = lax.broadcasted_iota(jnp.int32, (NTH, LANES), 0)
    cosine = jnp.full((NTH, LANES), COSINES[0], jnp.float32)
    sine = jnp.full((NTH, LANES), SINES[0], jnp.float32)
    for a in range(1, NTH):
        cosine = jnp.where(heading == a, COSINES[a], cosine)
        sine = jnp.where(heading == a, SINES[a], sine)
    for g in range(GROUPS):
        speed = SPEED_BASE + jnp.where(low_half, g, g + GROUPS).astype(jnp.float32) * SPEED_STEP
        table[0, :, lanes_of(g)] = cosine * speed * POS
        table[1, :, lanes_of(g)] = sine * speed * POS

    def split(vals):
        half = GROUPS // 2
        turned = [pltpu.roll(v, NW, 1) for v in vals]
        result = []
        for m in range(half):
            result.append(jnp.where(low_half, vals[m], turned[m + half]))
            result.append(jnp.where(low_half, turned[m], vals[m + half]))
        return result

    def joined(vals):
        half = GROUPS // 2
        turned = [pltpu.roll(v, NW, 1) for v in vals]
        return ([jnp.where(low_half, vals[2 * m], turned[2 * m + 1]) for m in range(half)]
                + [jnp.where(low_half, turned[2 * m], vals[2 * m + 1]) for m in range(half)])

    def row_slope(vals, tops):
        return tuple(
            functools.reduce(jnp.maximum, [jnp.abs(vals[g + 1] - vals[g]) for g in range(n, GROUPS - 1, len(tops))], top)
            for n, top in enumerate(tops))

    def seam_slope(step, tops):
        best = [zero, zero]
        for i in range(bx):
            for j in range(by):
                first = vb[step, i + 1, j + 1, :, lanes_of(0)]
                last = vb[step, i + 1, j + 1, :, lanes_of(GROUPS - 1)]
                best[j % 2] = jnp.maximum(best[j % 2], jnp.abs(pltpu.roll(first, NW, 1) - last))
        seam = jnp.where(low_half, jnp.maximum(best[0], best[1]), 0.0)
        return jnp.maximum(functools.reduce(jnp.maximum, tops), seam)

    for copy in loads:
        copy.wait()

    def first_rows(j, tops):
        rows = [split([nat_v[i, j, :, lanes_of(g)] for g in range(GROUPS)]) for i in range(bx)]
        for i, vals in enumerate(rows):
            for g in range(GROUPS):
                vb[0, i + 1, j + 1, :, lanes_of(g)] = vals[g]
            tops = row_slope(vals, tops)
        return tops

    top = seam_slope(0, lax.fori_loop(0, by, first_rows, (zero,) * 4))

    drift_copy.wait()
    east_ends = jnp.where(low_half, table[0, :, lanes_of(0)], table[0, :, lanes_of(GROUPS - 1)])
    north_ends = jnp.where(low_half, table[1, :, lanes_of(0)], table[1, :, lanes_of(GROUPS - 1)])
    best = [zero] * 2
    for i in range(bx):
        for j in range(by):
            both = jnp.abs(east_ends + drift[i, 0, j] * POS) + jnp.abs(north_ends + drift[i, 1, j] * POS)
            best[j % 2] = jnp.maximum(best[j % 2], both)
    local_rate[...] = jnp.maximum(best[0], best[1])

    def split_obstacle(j, carry):
        for i in range(bx):
            vals = split([nat_o[i, j, :, lanes_of(g)] for g in range(GROUPS)])
            for g in range(GROUPS):
                ob[i + 1, j + 1, :, lanes_of(g)] = vals[g]
        return carry

    pl.semaphore_wait(ready, jnp.where(beside_exists, 1, 0) + others + 1)

    def rim_copy(ref, at, side):
        inner = {0: (1, pl.ds(1, by)), 1: (bx, pl.ds(1, by)), 2: (pl.ds(1, bx), 1), 3: (pl.ds(1, bx), by)}[side]
        outer = {0: (bx + 1, pl.ds(1, by)), 1: (0, pl.ds(1, by)), 2: (pl.ds(1, bx), by + 1), 3: (pl.ds(1, bx), 0)}[side]
        return pltpu.make_async_remote_copy(
            src_ref=ref.at[inner], dst_ref=ref.at[outer],
            send_sem=halo_send.at[at, side], recv_sem=halo_recv.at[at, side],
            device_id=sides[side][1], device_id_type=MESH)

    def send_rims(ref, at):
        for side in (2, 3, 0, 1):
            @pl.when(sides[side][0])
            def _(side=side):
                rim_copy(ref, at, side).start()

    def take_rims(ref, at):
        for side in range(4):
            @pl.when(sides[side][0])
            def _(side=side):
                rim_copy(ref, at, opposite[side]).wait_recv()

    def ghost(step, side):
        if side < 2:
            to, near, far = ((0, 1, 2), (bx + 1, bx, bx - 1))[side]

            def fill(j, carry):
                vb[step, to, j] = 2.0 * vb[step, near, j] - vb[step, far, j]
                return carry

            lax.fori_loop(1, by + 1, fill, 0)
        else:
            to, near, far = ((0, 1, 2), (by + 1, by, by - 1))[side - 2]

            def fill(i, carry):
                vb[step, i, to] = 2.0 * vb[step, i, near] - vb[step, i, far]
                return carry

            lax.fori_loop(1, bx + 1, fill, 0)

    send_rims(vb.at[0], 0)

    def pair_copy(step):
        return pltpu.make_async_remote_copy(
            src_ref=pair.at[step, 0], dst_ref=pair.at[step, 1],
            send_sem=pair_send.at[step], recv_sem=pair_recv.at[step],
            device_id=partner, device_id_type=MESH)

    def spread(step):
        def send(n, peer):
            pltpu.make_async_remote_copy(
                src_ref=sent.at[step], dst_ref=got.at[step, n],
                send_sem=max_send.at[step], recv_sem=max_recv.at[step],
                device_id=peer, device_id_type=MESH).start()

        for_others(send)

    def wait_all(step, sem):
        rows = got.at[step, pl.ds(0, others)]
        pltpu.make_async_copy(rows, rows, sem.at[step]).wait()

    def largest(step, at):
        best = [sent[step, at]] + [got[step, n, at] for n in range(7)]
        for n in range(7, others):
            best[n % 8] = jnp.maximum(best[n % 8], got[step, n, at])
        return functools.reduce(jnp.maximum, best)

    def speed_sides(vals):
        seam_up = pltpu.roll(vals[0], NW, 1)
        seam_down = pltpu.roll(vals[GROUPS - 1], NW, 1)
        result = []
        for g, v in enumerate(vals):
            ahead = vals[g + 1] - v if g < GROUPS - 1 else seam_up - v
            behind = vals[g - 1] - v if g > 0 else seam_down - v
            if g == 0:
                behind = jnp.where(low_half, -ahead, behind)
            if g == GROUPS - 1:
                ahead = jnp.where(low_half, ahead, -behind)
            result.append((ahead, behind))
        return result

    def inner_terms(step):
        def row(i, j):
            vals = [vb[step, i, j, :, lanes_of(g)] for g in range(GROUPS)]
            for g, (ahead, behind) in enumerate(speed_sides(vals)):
                v = vals[g]
                span = ahead - behind
                part_b[i - 1, j - 1, :, lanes_of(g)] = ahead + behind
                acc = span * span * (1.0 / (4.0 * SPEED_STEP * SPEED_STEP * 2.0 * EFFORT_COST * SCALE))
                right = pltpu.roll(v, LANES - 1, 1) - v
                left = pltpu.roll(v, 1, 1) - v
                acc += jnp.maximum(jnp.where(last_turn, -left, right), jnp.where(first_turn, -right, left))
                around = jnp.where(turn_up, pltpu.roll(v, NTH - 1, 0), pltpu.roll(v, 1, 0))
                acc += turn_w * (around - v)
                part_a[step, i, j, :, lanes_of(g)] = acc

        return row

    def position_terms(step):
        def row(i, j):
            dx = drift[i - 1, 0, j - 1] * POS
            dy = drift[i - 1, 1, j - 1] * POS
            for g in range(GROUPS):
                s = lanes_of(g)
                v = vb[step, i, j, :, s]
                east = table[0, :, s] + dx
                north = table[1, :, s] + dy
                from_x = jnp.where(east > 0.0, vb[step, i + 1, j, :, s], vb[step, i - 1, j, :, s])
                from_y = jnp.where(north > 0.0, vb[step, i, j + 1, :, s], vb[step, i, j - 1, :, s])
                part_a[step, i, j, :, s] += jnp.abs(east) * (from_x - v) + jnp.abs(north) * (from_y - v)

        return row

    def each(first, last, rows):
        def body(j, carry):
            rows(j)
            return carry

        lax.fori_loop(first, last, body, 0)

    def halo_row(step, i, j):
        before = step - 1
        vals = [vb[before, i, j, :, lanes_of(g)] for g in range(GROUPS)]
        for g, (ahead, behind) in enumerate(speed_sides(vals)):
            s = lanes_of(g)
            moved = vals[g] + held[0] * part_a[before, i, j, :, s] + held[1] * (ahead + behind)
            vb[step, i, j, :, s] = jnp.minimum(moved, ob[i, j, :, s])

    def halo_rows(step):
        for side, i in ((0, 0), (1, bx + 1)):
            @pl.when(sides[side][0])
            def _(i=i):
                def pair_of_rows(n):
                    halo_row(step, i, 2 * n + 1)
                    halo_row(step, i, 2 * n + 2)

                each(0, by // 2, pair_of_rows)

        for side, j in ((2, 0), (3, by + 1)):
            @pl.when(sides[side][0])
            def _(j=j):
                def pair_of_rows(n):
                    halo_row(step, 2 * n + 1, j)
                    halo_row(step, 2 * n + 2, j)

                each(0, bx // 2, pair_of_rows)

    def share(step, top):
        inner, position = inner_terms(step), position_terms(step)
        pair[step, 0, 0] = top
        pair[step, 0, 1] = local_rate[...]
        pair_copy(step).start()

        def inner_rows(planes):
            def rows(j):
                for i in planes:
                    inner(i, j)

            return rows

        def y_rim_rows(n):
            for i in range(1, bx + 1):
                inner(i, n * (by - 1) + 1)

        def x_rim_rows(j):
            inner(1, j)
            inner(bx, j)

        each(0, 2, y_rim_rows)
        each(2, 4, x_rim_rows)
        pair_copy(step).wait_recv()
        sent[step, 0] = jnp.max(jnp.maximum(pair[step, 0, 0], pair[step, 1, 0]))

        @pl.when(step == 0)
        def _():
            rates[0] = jnp.max(jnp.maximum(pair[step, 0, 1], pair[step, 1, 1]))

        sent[step, 1] = rates[0]
        spread(step)

        each(4, by, x_rim_rows)

        @pl.when(step == 0)
        def _():
            ob_copy.wait()
            each(0, by, lambda j: split_obstacle(j, 0))
            send_rims(ob, ITERS)
            take_rims(vb.at[0], 0)

        @pl.when(step == 1)
        def _():
            take_rims(ob, ITERS)

        @pl.when(step > 0)
        def _():
            take_rims(part_a.at[step - 1], step)
            halo_rows(step)

        for side in range(4):
            @pl.when(jnp.logical_not(sides[side][0]))
            def _(side=side):
                ghost(step, side)

        def x_rims(j):
            position(1, j)
            position(bx, j)

        def y_rims(i):
            position(i, 1)
            position(i, by)

        def inside(j):
            for i in range(2, bx):
                position(i, j)

        each(1, by + 1, x_rims)
        each(2, bx, y_rims)

        @pl.when(step < ITERS - 1)
        def _():
            send_rims(part_a.at[step], step + 1)

        each(2, by, inner_rows(range(2, bx)))
        each(2, by, inside)

    def weights(step):
        wait_all(step, max_recv)
        slope = largest(step, 0)

        @pl.when(step == 0)
        def _():
            rates[0] = largest(step, 1)

        top_slope = jnp.full((NTH, LANES), slope, jnp.float32) * (1.0 / SPEED_STEP)
        rate_top = jnp.full((NTH, LANES), rates[0], jnp.float32) * SCALE + TURN_TOP + SCALE
        dt = COURANT / (rate_top + top_slope * (1.0 / (EFFORT_COST * SPEED_STEP)))
        times[step] = dt
        held[0] = SCALE * dt
        held[1] = dt * top_slope * (0.5 / (SPEED_STEP * EFFORT_COST))
        return held[0], held[1]

    def one_step(step, top):
        share(step, top)
        weight_a, weight_b = weights(step)

        def update(n, tops):
            for i, j in [(i, 4 * n + m) for m in (1, 2, 3, 4) for i in range(1, bx + 1)]:
                vals = []
                for g in range(GROUPS):
                    s = lanes_of(g)
                    moved = vb[step, i, j, :, s] + weight_a * part_a[step, i, j, :, s] + weight_b * part_b[i - 1, j - 1, :, s]
                    moved = jnp.minimum(moved, ob[i, j, :, s])
                    vb[step + 1, i, j, :, s] = moved
                    vals.append(moved)
                tops = row_slope(vals, tops)
            return tops

        tops = lax.fori_loop(0, by // 4, update, (zero,) * 4)
        return seam_slope(step + 1, tops)

    top = lax.fori_loop(0, ITERS - 1, one_step, top)
    last = ITERS - 1
    share(last, top)

    weight_a, weight_b = weights(last)
    stores = []
    half = by // 2
    for i in range(bx):
        def final(part, carry, i=i):
            for n in range(half):
                j = part * half + n
                vals = []
                for g in range(GROUPS):
                    s = lanes_of(g)
                    vals.append(vb[last, i + 1, j + 1, :, s] + weight_a * part_a[last, i + 1, j + 1, :, s]
                                + weight_b * part_b[i, j, :, s])
                for g, moved in enumerate(joined(vals)):
                    nat_v[i, j, :, lanes_of(g)] = jnp.minimum(moved, nat_o[i, j, :, lanes_of(g)])
            return carry

        lax.fori_loop(0, 2, final, 0)
        copy = pltpu.make_async_copy(nat_v.at[i], out_hbm.at[i], out_sem.at[i])
        copy.start()
        stores.append(copy)

    for step in range(ITERS):
        steps_out[step] = jnp.max(times[step])

    def finish(step, carry):
        pair_copy(step).wait_send()
        wait_all(step, max_send)
        return carry

    lax.fori_loop(0, ITERS, finish, 0)

    def rims_sent(at, carry):
        for side in range(4):
            @pl.when(sides[side][0])
            def _(side=side):
                rim_copy(ob, at, side).wait_send()
        return carry

    lax.fori_loop(0, ITERS + 1, rims_sent, 0)
    for copy in stores:
        copy.wait()


def per_device(nx, ny, value_field, obstacle, drift_field):
    bx, by = value_field.shape[:2]
    shape = value_field.shape
    hbm = pl.BlockSpec(memory_space=pltpu.MemorySpace.HBM)
    dma = pltpu.SemaphoreType.DMA
    block = pltpu.VMEM(shape, jnp.float32)
    return pl.pallas_call(
        functools.partial(kernel, nx, ny, bx, by),
        out_shape=(jax.ShapeDtypeStruct(shape, jnp.float32), jax.ShapeDtypeStruct((ITERS,), jnp.float32)),
        in_specs=[hbm, hbm, hbm],
        out_specs=(pl.BlockSpec(memory_space=pl.ANY), pl.BlockSpec(memory_space=pltpu.SMEM)),
        scratch_shapes=[
            pltpu.VMEM((ITERS, bx + 2, by + 2) + shape[2:], jnp.float32),
            block, block,
            pltpu.VMEM((bx + 2, by + 2) + shape[2:], jnp.float32),
            pltpu.VMEM((ITERS, bx + 2, by + 2) + shape[2:], jnp.float32),
            block,
            pltpu.VMEM((2,) + shape[2:], jnp.float32),
            pltpu.SMEM((bx, 2, by), jnp.float32),
            pltpu.VMEM((ITERS, 2, 2, NTH, LANES), jnp.float32),
            pltpu.SMEM((ITERS, 8), jnp.float32),
            pltpu.SMEM((ITERS, ny * len(PLANE) - 1, 8), jnp.float32),
            pltpu.SMEM((1,), jnp.float32),
            pltpu.VMEM((NTH, LANES), jnp.float32),
            pltpu.VMEM((ITERS, NTH, LANES), jnp.float32),
            pltpu.VMEM((2, NTH, LANES), jnp.float32),
            dma((bx,)), dma, dma, dma((bx,)),
            dma((ITERS + 1, 4)), dma((ITERS + 1, 4)), dma((ITERS,)), dma((ITERS,)), dma((ITERS,)), dma((ITERS,)),
        ],
        compiler_params=pltpu.CompilerParams(
            collective_id=0, has_side_effects=True, vmem_limit_bytes=52 * 1024 * 1024),
        name="safe_set_steps",
    )(pltpu.with_memory_space_constraint(jnp.transpose(drift_field, (0, 2, 1)), pltpu.MemorySpace.HBM), value_field, obstacle)


def solution(mesh):
    nx, ny = mesh.shape["gx"], mesh.shape["gy"]
    placed = (P("gx", "gy", None, None), P("gx", "gy", None, None), P("gx", "gy", None))
    return jax.shard_map(
        functools.partial(per_device, nx, ny),
        mesh=mesh,
        in_specs=placed,
        out_specs=(P("gx", "gy", None, None), P()),
        check_vma=False,
    )
```
